32 devices in a mesh: chan: 4 (over y, core), inp: 8 (over z, x).
Axes of the slice: x: 2, y: 2, z: 4, core: 2. Of those that a mesh axis runs over, the one named last changes fastest.
Arguments:
- voltages: bfloat16 [1024, 131072], P('inp', 'chan'), may hold values from -64 to 64
- tile_table: int32 [40, 2], replicated, may hold values from -1 to 7, as said below
Outputs:
- coherence: float32 [512, 40, 128, 256], P('chan', 'inp')
The draws below stay inside these ranges and needn't reach their ends.
Inputs may be any that keep to these rules, and one draw needn't show every extreme that they name: `tile_table`: rows 5 d to 5 d + 4 are the slots whose tiles the device at index d along inp outputs. Every pair (a, b) with 0 <= a <= b < 8 stands in exactly one row, and every other row is (-1, -1); the pairs are spread over the rows in any order.
All inputs are finite; a program needn't handle non-finite values.
Results may differ from the reference program's by a relative error of at most 0.0058.
Values may be sent and summed in bfloat16 or wider, within the bound.
A program may use at most 256 MiB of HBM per device.

```python
import math
import jax
import jax.numpy as jnp
import numpy as np
from jax import lax

NI = 1024
L = 2048
NCH = 512
TAPS = 4
NB = 128
FRAMES = 64
NSAMP = 131072
N_INP = 8


def draw_voltages(key, part):
    key_noise = jax.random.fold_in(key, 0)
    thermal = jax.random.normal(key_noise, (NI, NSAMP), jnp.float32)
    values = thermal
    return jnp.clip(values, -64.0, 64.0).astype(jnp.bfloat16)


def draw_tile_table(key, part):
    tile_count = N_INP * (N_INP + 1) // 2
    slot_count = N_INP * (N_INP // 2 + 1)
    upper_rows, upper_cols = np.triu_indices(N_INP)
    pair_list = np.concatenate([np.stack([upper_rows, upper_cols], axis=1), -np.ones((slot_count - tile_count, 2), np.int64)], axis=0)
    pair_list = jnp.asarray(pair_list.astype(np.int32))
    shuffle = jax.random.permutation(key, slot_count)
    return pair_list[shuffle]


def setup_inputs(seed: int = 0) -> dict:
    keys = jax.random.split(jax.random.key(seed), 3)
    return {
        "voltages": draw_voltages(jax.random.fold_in(keys[2], 71), 0),
        "tile_table": draw_tile_table(jax.random.fold_in(keys[2], 71), 0),
    }


def filter_window():
    positions = jnp.arange(TAPS * L, dtype=jnp.float32)
    shape_sinc = jnp.sinc((positions - TAPS * L / 2.0) / L)
    tapering = 0.5 - 0.5 * jnp.cos(2.0 * math.pi * positions / (TAPS * L))
    return (shape_sinc * tapering).reshape(TAPS, L)

def transform_table():
    samples = jnp.arange(L, dtype=jnp.int32)[:, None]
    channels = jnp.arange(NCH, dtype=jnp.int32)[None, :]
    phases = samples * channels % L
    angles = phases.astype(jnp.float32) * (2.0 * math.pi / L)
    return jnp.stack([jnp.cos(angles), -jnp.sin(angles)], axis=2).reshape(L, 2 * NCH).astype(jnp.bfloat16)

def rotate_parts(rows):
    half_width = rows.shape[-1] // 2
    return jnp.concatenate([-rows[..., half_width:], rows[..., :half_width]], axis=-1)

def channel_tiles(columns, channel_power, first_all, second_all, present_all, block_width, frame_total):
    partner = jnp.concatenate([columns, rotate_parts(columns)], axis=0)
    gram_full = lax.dot_general(columns, partner, (((1,), (1,)), ((), ())), preferred_element_type=jnp.float32)
    block_count = columns.shape[0] // block_width
    gram_grid = gram_full.reshape(block_count, block_width, 2, block_count, block_width)
    picked = gram_grid[first_all, :, :, second_all, :]
    picked = picked.reshape(first_all.shape[0], block_width, 2 * block_width)
    power_grid = channel_power.reshape(block_count, block_width)
    inverse = present_all[:, None, None] / (frame_total * jnp.sqrt(power_grid[first_all][:, :, None] * power_grid[second_all][:, None, :]))
    return picked * jnp.concatenate([inverse, inverse], axis=2)

def reference(voltages, tile_table):
    blocks = voltages.reshape(NI, FRAMES, L)
    extended = jnp.concatenate([blocks, jnp.zeros((NI, TAPS - 1, L), voltages.dtype)], axis=1)
    window = filter_window()
    filtered = jnp.zeros((NI, FRAMES, L), jnp.float32)
    for tap_index in range(TAPS):
        filtered = filtered + extended[:, tap_index:tap_index + FRAMES, :].astype(jnp.float32) * window[tap_index]
    filtered = filtered.astype(jnp.bfloat16).reshape(NI * FRAMES, L)
    spectra = jnp.dot(filtered, transform_table(), preferred_element_type=jnp.float32).astype(jnp.bfloat16)
    arranged = spectra.reshape(NI, FRAMES, NCH, 2).transpose(2, 0, 3, 1).reshape(NCH, NI, 2 * FRAMES)
    autopower = lax.optimization_barrier(jnp.sum(jnp.square(arranged.astype(jnp.float32)), axis=2)) / FRAMES + 1e-06
    first_all = jnp.maximum(tile_table[:, 0], 0).astype(jnp.int32)
    second_all = jnp.maximum(tile_table[:, 1], 0).astype(jnp.int32)
    present_all = (tile_table[:, 0] >= 0).astype(jnp.float32)

    def per_channel(pair_in):
        return channel_tiles(pair_in[0], pair_in[1], first_all, second_all, present_all, NB, FRAMES)
    return lax.map(per_channel, (arranged, autopower))
```

```python
import functools
import math

import jax
import jax.numpy as jnp
import ml_dtypes
import numpy as np
from jax import lax
from jax.experimental import pallas as pl
from jax.experimental.pallas import tpu as pltpu
from jax.sharding import PartitionSpec as P

L = 2048
NCH = 512
TAPS = 4
PAIR = 2
PARTS = 2
LOADS = 4
MESH = pl.DeviceIdType.MESH


def filter_window():
    positions = np.arange(TAPS * L, dtype=np.float64)
    shape_sinc = np.sinc((positions - TAPS * L / 2.0) / L)
    tapering = 0.5 - 0.5 * np.cos(2.0 * math.pi * positions / (TAPS * L))
    return (shape_sinc * tapering).reshape(TAPS, L).astype(np.float32)


def transform_rows():
    channels, samples = np.arange(NCH)[:, None], np.arange(L)[None, :]
    angles = (channels * samples % L) * (2.0 * math.pi / L)
    both = np.stack([np.cos(angles), -np.sin(angles)], axis=1)
    return both.reshape(2 * NCH, L).astype(ml_dtypes.bfloat16)


def flipped(group, mask, groups):
    result, bit = group, 1
    while bit < groups:
        result = result + (mask // bit % 2) * bit * (1 - 2 * (group // bit % 2))
        bit *= 2
    return result


def spectra_kernel(sizes, volt_ref, rows_ref, window_ref, all_ref, *scratch):
    rows, columns, groups, crossed = sizes
    extended, filtered, table, total, own = scratch[:5]
    load_sem, table_sem, halo_sem, local_sem = scratch[5:9]
    send_line, send_cross, recv_sem, turn_send, turn_recv = scratch[9:]
    width, local_len = volt_ref.shape
    frames = local_len // L
    halo_len = (TAPS - 1) * L
    channels, depth = own.shape[0] // groups, own.shape[1]
    group_rows = 2 * channels
    step = channels // PARTS
    chunks = 2 + (groups - 1) * PARTS
    me, group = lax.axis_index("inp"), lax.axis_index("chan")
    has_next, has_last = group < groups - 1, group > 0
    z, x = me // columns, me % columns
    up = ("up", 0, z < rows - 1, me + columns)
    down = ("down", 1, z > 0, me - columns)
    right = ("right", 2, x < columns - 1, me + 1)
    left = ("left", 3, x > 0, me - 1)
    along_z, along_x = (up, down), (right, left)
    part_rows = width // LOADS

    def load(index):
        place = pl.ds(pl.multiple_of(index * part_rows, part_rows), part_rows)
        return pltpu.make_async_copy(
            volt_ref.at[place], extended.at[place, pl.ds(0, local_len)], load_sem.at[index]
        )

    def load_rows(mask):
        first = pl.multiple_of(flipped(group, mask, groups) * group_rows, group_rows)
        place = pl.ds(first, group_rows)
        return pltpu.make_async_copy(rows_ref.at[place], table.at[place], table_sem.at[mask])

    for index in range(LOADS):
        load(index).start()
    for mask in range(groups):
        load_rows(mask).start()

    barrier = pltpu.get_barrier_semaphore()
    expected = jnp.int32(groups - 1)
    for mask in range(1, groups):
        target = flipped(group, mask, groups)
        pl.semaphore_signal(barrier, inc=1, device_id={"chan": target}, device_id_type=MESH)
    for _, _, exists, target in along_z + along_x:
        expected = expected + exists.astype(jnp.int32)

        @pl.when(exists)
        def _(target=target):
            pl.semaphore_signal(barrier, inc=1, device_id={"inp": target}, device_id_type=MESH)

    pl.semaphore_wait(barrier, expected)
    halo = pltpu.make_async_remote_copy(
        src_ref=volt_ref.at[:, pl.ds(0, halo_len)],
        dst_ref=extended.at[:, pl.ds(local_len, halo_len)],
        send_sem=halo_sem.at[0],
        recv_sem=halo_sem.at[1],
        device_id={"chan": group - 1},
        device_id_type=MESH,
    )

    @pl.when(has_last)
    def _():
        halo.start()

    @pl.when(jnp.logical_not(has_next))
    def _():
        extended[:, pl.ds(local_len, halo_len)] = jnp.zeros((width, halo_len), jnp.bfloat16)

    strip, lanes = 16, 256

    def filter_frames(first, last, row_first, row_last):
        def column(index, carry):
            start = pl.multiple_of(index * lanes, lanes)
            weights = [window_ref[tap : tap + 1, pl.ds(start, lanes)] for tap in range(TAPS)]

            def samples(place, frame):
                return extended[place, pl.ds(frame * L + start, lanes)].astype(jnp.float32)

            def one_strip(row, carry):
                place = pl.ds(pl.multiple_of(row * strip, strip), strip)
                held = [samples(place, first + tap) for tap in range(TAPS - 1)]
                for frame in range(first, last):
                    held.append(samples(place, frame + TAPS - 1))
                    value = held[0] * weights[0]
                    for tap in range(1, TAPS):
                        value = value + held[tap] * weights[tap]
                    to = pl.ds(pl.multiple_of(frame * width + row * strip, strip), strip)
                    filtered[to, pl.ds(start, lanes)] = value.astype(jnp.bfloat16)
                    held = held[1:]
                return carry

            lax.fori_loop(row_first, row_last, one_strip, jnp.int32(0))
            return carry

        lax.fori_loop(0, L // lanes, column, jnp.int32(0))

    dot_rows = min(256, group_rows)

    def transform(mask, first, last):
        start = flipped(group, mask, groups) * group_rows

        def one(pair, carry):
            taken = pl.ds(pl.multiple_of(pair * PAIR * width, PAIR * width), PAIR * width)
            for row in range(0, group_rows, dot_rows):
                place = pl.ds(pl.multiple_of(start + row, dot_rows), dot_rows)
                product = lax.dot_general(
                    table[place, :],
                    filtered[taken, :],
                    (((1,), (1,)), ((), ())),
                    preferred_element_type=jnp.float32,
                )
                for inner in range(PAIR):
                    base = (mask * group_rows + row) * frames + pair * PAIR + inner
                    where = pl.ds(base, dot_rows, stride=frames)
                    total[where, :] = product[:, inner * width : (inner + 1) * width]
            return carry

        lax.fori_loop(first, last, one, jnp.int32(0))

    def put(mask):
        first = flipped(group, mask, groups) * channels
        some = 8

        def one(index, carry):
            taken = pl.ds(
                pl.multiple_of((mask * channels + index * some) * depth, some * depth), some * depth
            )
            own[pl.ds(first + index * some, some)] = (
                total[taken, :].reshape(some, depth, width).astype(jnp.bfloat16)
            )
            return carry

        lax.fori_loop(0, channels // some, one, jnp.int32(0))

    def where(chunk):
        if isinstance(chunk, int) and chunk < 2:
            return 0, chunk * crossed, (channels - crossed if chunk else crossed)
        return 1 + (chunk - 2) // PARTS, (chunk - 2) % PARTS * step, step

    def rows_of(block, first, count, time):
        return all_ref.at[
            block, pl.ds(first, count), pl.ds(pl.multiple_of(time * depth, depth), depth)
        ]

    def part(block, chunk):
        mask, first, count = where(chunk)
        return rows_of(block, first, count, flipped(group, mask, groups))

    def own_part(chunk):
        mask, first, count = where(chunk)
        return own.at[pl.ds(flipped(group, mask, groups) * channels + first, count)]

    def turn(chunk, arriving=False):
        mask, first, count = where(chunk)
        return pltpu.make_async_remote_copy(
            src_ref=own_part(chunk),
            dst_ref=part(me, chunk) if arriving else rows_of(me, first, count, group),
            send_sem=turn_send.at[chunk],
            recv_sem=turn_recv.at[chunk],
            device_id={"chan": flipped(group, mask, groups)},
            device_id_type=MESH,
        )

    def copy(block, chunk, way, to_sems, source=None):
        place = part(block, chunk)
        return pltpu.make_async_remote_copy(
            src_ref=place if source is None else source,
            dst_ref=place,
            send_sem=to_sems.at[way[1], block],
            recv_sem=recv_sem.at[block, chunk],
            device_id={"inp": way[3]},
            device_id_type=MESH,
        )

    def send(block, chunk, ways, to_sems, source=None):
        for way in ways:

            @pl.when(way[2])
            def _(way=way):
                copy(block, chunk, way, to_sems, source).start()

    def pass_on(block, chunk, exists, ways, to_sems, origin):
        @pl.when(exists)
        def _():
            copy(block, chunk, origin, to_sems).wait_recv()
            send(block, chunk, ways, to_sems)

    def over(first, last, body):
        def one(chunk, carry):
            body(chunk)
            return carry

        for chunk in range(first, min(last, 2)):
            body(chunk)
        if last > 2:
            lax.fori_loop(max(first, 2), last, one, jnp.int32(0))

    def of_mask(mask):
        return (1, 2) if mask == 0 else (2 + (mask - 1) * PARTS, 2 + mask * PARTS)

    store = pltpu.make_async_copy(
        own.at[pl.ds(group * channels, channels)],
        all_ref.at[me, :, pl.ds(pl.multiple_of(group * depth, depth), depth)],
        local_sem,
    )

    def launch(mask):
        if mask:
            over(*of_mask(mask), lambda c: turn(c).start())
        else:
            send(me, 0, along_x + along_z, send_cross, own_part(0))
            send(me, 1, along_z + along_x, send_line, own_part(1))
            store.start()

    clear = max(0, (frames - TAPS + 1) // PAIR)
    early = min(2, groups)

    def loaded(index, carry):
        load(index).wait()
        many = part_rows // strip
        filter_frames(0, clear * PAIR, index * many, (index + 1) * many)
        return carry

    lax.fori_loop(0, LOADS, loaded, jnp.int32(0))
    for mask in range(early):
        load_rows(mask).wait()
        transform(mask, 0, clear)

    @pl.when(has_next)
    def _():
        halo.wait_recv()

    filter_frames(clear * PAIR, frames, 0, width // strip)
    for mask in range(groups):
        if mask >= early:
            load_rows(mask).wait()
        transform(mask, clear if mask < early else 0, frames // PAIR)
        put(mask)
        launch(mask)

    def own_turned(mask):
        def one(chunk):
            turn(chunk, True).wait_recv()
            send(me, chunk, along_z + along_x, send_line)

        over(*of_mask(mask), one)

    def line(away, first, last):
        below, above = z >= away, z + away < rows

        def one(chunk):
            pass_on(me - away * columns, chunk, below, along_x + (up,), send_line, down)
            pass_on(me + away * columns, chunk, above, along_x + (down,), send_line, up)

        over(first, last, one)

    def crossing(away):
        below, above = z >= away, z + away < rows
        for column in range(columns):
            low = (z - away) * columns + column
            high = (z + away) * columns + column
            pass_on(low, 0, below, (up,), send_cross, down)
            pass_on(high, 0, above, (down,), send_cross, up)

    for away in range(1, columns):
        pass_on(me - away, 0, x >= away, (right,) + along_z, send_cross, left)
        pass_on(me + away, 0, x + away < columns, (left,) + along_z, send_cross, right)
    own_turned(1)
    crossing(1)
    line(1, *of_mask(0))
    for mask in range(2, groups):
        own_turned(mask)
        line(1, *of_mask(mask - 1))
    line(1, *of_mask(groups - 1))
    for away in range(2, rows):
        crossing(away)
        line(away, 1, chunks)
    for away in range(1, columns):
        for row in range(rows):
            before = row * columns + x - away
            after = row * columns + x + away

            def across(chunk):
                pass_on(before, chunk, x >= away, (right,), send_line, left)
                pass_on(after, chunk, x + away < columns, (left,), send_line, right)

            over(1, chunks, across)

    def drain(block, way, cond, to_sems, count):
        @pl.when(jnp.logical_and(cond, way[2]))
        def _():
            whole = all_ref.at[block, pl.ds(0, count)]
            pltpu.make_async_remote_copy(
                src_ref=whole,
                dst_ref=whole,
                send_sem=to_sems.at[way[1], block],
                recv_sem=recv_sem.at[block, 0],
                device_id={"inp": way[3]},
                device_id_type=MESH,
            ).wait_send()

    for row in range(rows):
        for column in range(columns):
            block = row * columns + column
            here, same = x == column, z == row
            drain(block, up, jnp.logical_and(here, z >= row), send_line, channels - crossed // groups)
            drain(block, down, jnp.logical_and(here, z <= row), send_line, channels - crossed // groups)
            drain(block, right, x >= column, send_line, channels - crossed // groups)
            drain(block, left, x <= column, send_line, channels - crossed // groups)
            drain(block, up, z >= row, send_cross, crossed // groups)
            drain(block, down, z <= row, send_cross, crossed // groups)
            drain(block, right, jnp.logical_and(same, x >= column), send_cross, crossed // groups)
            drain(block, left, jnp.logical_and(same, x <= column), send_cross, crossed // groups)
    over(2, chunks, lambda c: turn(c).wait_send())
    store.wait()

    @pl.when(has_last)
    def _():
        halo.wait_send()


def gathered_spectra(voltages):
    width, local_len = voltages.shape
    frames = local_len // L
    devices, groups = lax.axis_size("inp"), lax.axis_size("chan")
    columns = 1 << (int(math.log2(devices)) // 2)
    rows = devices // columns
    channels, depth = NCH // groups, 2 * frames
    chunks = 2 + (groups - 1) * PARTS
    share = ((columns - 1) * rows - rows + 1) / (2 * (rows - 1) * (columns - 1))
    crossed = min(int(0.94 * share * groups * channels), channels - 16) // 16 * 16
    return pl.pallas_call(
        functools.partial(spectra_kernel, (rows, columns, groups, crossed)),
        out_shape=jax.ShapeDtypeStruct((devices, channels, groups * depth, width), jnp.bfloat16),
        in_specs=[
            pl.BlockSpec(memory_space=pl.ANY),
            pl.BlockSpec(memory_space=pl.ANY),
            pl.BlockSpec(memory_space=pltpu.VMEM),
        ],
        out_specs=pl.BlockSpec(memory_space=pl.ANY),
        scratch_shapes=[
            pltpu.VMEM((width, local_len + (TAPS - 1) * L), jnp.bfloat16),
            pltpu.VMEM((frames * width, L), jnp.bfloat16),
            pltpu.VMEM((2 * NCH, L), jnp.bfloat16),
            pltpu.VMEM((2 * NCH * frames, width), jnp.float32),
            pltpu.VMEM((NCH, depth, width), jnp.bfloat16),
            pltpu.SemaphoreType.DMA((LOADS,)),
            pltpu.SemaphoreType.DMA((groups,)),
            pltpu.SemaphoreType.DMA((2,)),
            pltpu.SemaphoreType.DMA,
            pltpu.SemaphoreType.DMA((4, devices)),
            pltpu.SemaphoreType.DMA((4, devices)),
            pltpu.SemaphoreType.DMA((devices, chunks)),
            pltpu.SemaphoreType.DMA((chunks,)),
            pltpu.SemaphoreType.DMA((chunks,)),
        ],
        compiler_params=pltpu.CompilerParams(
            collective_id=0, has_side_effects=True, vmem_limit_bytes=52 << 20
        ),
        name="spectra",
    )(voltages, jnp.asarray(transform_rows()), jnp.asarray(filter_window()))


def tile_kernel(slots, frames, groups, table_ref, all_ref, out_ref):
    depth = all_ref.shape[2]
    local = depth // (2 * groups)

    def scaled(block, channel):
        rows = all_ref[block, channel].astype(jnp.float32)
        autopower = jnp.sum(rows * rows, axis=0, keepdims=True) / frames + 1e-06
        return rows * (1.0 / (math.sqrt(frames) * jnp.sqrt(autopower)))

    def one(channel, carry):
        for slot in range(slots):
            first, second = table_ref[slot, 0], table_ref[slot, 1]
            left = scaled(jnp.maximum(first, 0), channel)
            left = jnp.where(first >= 0, left, jnp.zeros_like(left)).astype(jnp.bfloat16)
            right = scaled(jnp.maximum(second, 0), channel).astype(jnp.bfloat16)
            pieces = []
            for start in range(0, depth, 2 * local):
                pieces.append(-right[start + local : start + 2 * local])
                pieces.append(right[start : start + local])
            partner = jnp.concatenate([right, jnp.concatenate(pieces, axis=0)], axis=1)
            out_ref[channel, slot] = lax.dot_general(
                left, partner, (((0,), (0,)), ((), ())), preferred_element_type=jnp.float32
            )
        return carry

    lax.fori_loop(0, all_ref.shape[1], one, jnp.int32(0), unroll=2)


def make_tiles(everything, slot_rows):
    devices, channel_count, depth, width = everything.shape
    slots = slot_rows.shape[0]
    lanes = max(width, 128)
    block_bytes = 2 * devices * depth * lanes + 4 * slots * width * max(2 * width, 128)
    group = 16
    while 2 * group * block_bytes > 32 << 20:
        group //= 2
    return pl.pallas_call(
        functools.partial(tile_kernel, slots, depth // 2, lax.axis_size("chan")),
        out_shape=jax.ShapeDtypeStruct((channel_count, slots, width, 2 * width), jnp.float32),
        grid_spec=pltpu.PrefetchScalarGridSpec(
            num_scalar_prefetch=1,
            grid=(channel_count // group,),
            in_specs=[pl.BlockSpec((devices, group, depth, width), lambda c, t: (0, c, 0, 0))],
            out_specs=pl.BlockSpec((group, slots, width, 2 * width), lambda c, t: (c, 0, 0, 0)),
        ),
        compiler_params=pltpu.CompilerParams(vmem_limit_bytes=48 << 20),
        name="tiles",
    )(slot_rows, everything)


def on_device(voltages, tile_table):
    everything = gathered_spectra(voltages)
    slot_total = tile_table.shape[0] // lax.axis_size("inp")
    slot_rows = lax.dynamic_slice_in_dim(
        tile_table, lax.axis_index("inp") * slot_total, slot_total, 0
    )
    return make_tiles(everything, slot_rows)


def solution(mesh):
    placed = (P("inp", "chan"), P())
    return jax.shard_map(
        on_device,
        mesh=mesh,
        in_specs=placed,
        out_specs=P("chan", "inp", None, None),
        check_vma=False,
    )
```

```python
import functools
import math

import jax
import jax.numpy as jnp
import ml_dtypes
import numpy as np
from jax import lax
from jax.experimental import pallas as pl
from jax.experimental.pallas import tpu as pltpu
from jax.sharding import PartitionSpec as P

L = 2048
NCH = 512
TAPS = 4
PAIR = 2
PARTS = 2
LOADS = 4
MESH = pl.DeviceIdType.MESH


def filter_window():
    positions = np.arange(TAPS * L, dtype=np.float64)
    shape_sinc = np.sinc((positions - TAPS * L / 2.0) / L)
    tapering = 0.5 - 0.5 * np.cos(2.0 * math.pi * positions / (TAPS * L))
    return (shape_sinc * tapering).reshape(TAPS, L).astype(np.float32)


def transform_rows():
    channels, samples = np.arange(NCH)[:, None], np.arange(L)[None, :]
    angles = (channels * samples % L) * (2.0 * math.pi / L)
    both = np.stack([np.cos(angles), -np.sin(angles)], axis=1)
    return both.reshape(2 * NCH, L).astype(ml_dtypes.bfloat16)


def flipped(group, mask, groups):
    result, bit = group, 1
    while bit < groups:
        result = result + (mask // bit % 2) * bit * (1 - 2 * (group // bit % 2))
        bit *= 2
    return result


def spectra_kernel(sizes, volt_ref, rows_ref, window_ref, all_ref, *scratch):
    rows, columns, groups, crossed, line_tail, cross_tail = sizes
    tails = line_tail + cross_tail
    if tails:
        line_ref, cross_ref, outward_ref, *scratch = scratch
    extended, filtered, table, total, own = scratch[:5]
    load_sem, table_sem, halo_sem, local_sem = scratch[5:9]
    send_line, send_cross, recv_sem, turn_send, turn_recv = scratch[9:14]
    tail_sems = scratch[14:]
    width, local_len = volt_ref.shape
    frames = local_len // L
    halo_len = (TAPS - 1) * L
    channels, depth = own.shape[0] // groups, own.shape[1]
    group_rows = 2 * channels
    kept = channels - tails
    step = kept // PARTS
    chunks = 2 + (groups - 1) * PARTS
    me, group = lax.axis_index("inp"), lax.axis_index("chan")
    has_next, has_last = group < groups - 1, group > 0
    z, x = me // columns, me % columns
    up = ("up", 0, z < rows - 1, me + columns)
    down = ("down", 1, z > 0, me - columns)
    right = ("right", 2, x < columns - 1, me + 1)
    left = ("left", 3, x > 0, me - 1)
    along_z, along_x = (up, down), (right, left)
    at_end = jnp.logical_or(z == 0, z == rows - 1)
    inner_z = (("up", 0, z < rows - 2, me + columns), ("down", 1, z > 1, me - columns))
    part_rows = width // LOADS

    def load(index):
        place = pl.ds(pl.multiple_of(index * part_rows, part_rows), part_rows)
        return pltpu.make_async_copy(
            volt_ref.at[place], extended.at[place, pl.ds(0, local_len)], load_sem.at[index]
        )

    def load_rows(mask):
        first = pl.multiple_of(flipped(group, mask, groups) * group_rows, group_rows)
        place = pl.ds(first, group_rows)
        return pltpu.make_async_copy(rows_ref.at[place], table.at[place], table_sem.at[mask])

    for index in range(LOADS):
        load(index).start()
    for mask in range(groups):
        load_rows(mask).start()

    barrier = pltpu.get_barrier_semaphore()
    expected = jnp.int32(groups - 1)
    for mask in range(1, groups):
        target = flipped(group, mask, groups)
        pl.semaphore_signal(barrier, inc=1, device_id={"chan": target}, device_id_type=MESH)
    for _, _, exists, target in along_z + along_x:
        expected = expected + exists.astype(jnp.int32)

        @pl.when(exists)
        def _(target=target):
            pl.semaphore_signal(barrier, inc=1, device_id={"inp": target}, device_id_type=MESH)

    pl.semaphore_wait(barrier, expected)
    halo = pltpu.make_async_remote_copy(
        src_ref=volt_ref.at[:, pl.ds(0, halo_len)],
        dst_ref=extended.at[:, pl.ds(local_len, halo_len)],
        send_sem=halo_sem.at[0],
        recv_sem=halo_sem.at[1],
        device_id={"chan": group - 1},
        device_id_type=MESH,
    )

    @pl.when(has_last)
    def _():
        halo.start()

    @pl.when(jnp.logical_not(has_next))
    def _():
        extended[:, pl.ds(local_len, halo_len)] = jnp.zeros((width, halo_len), jnp.bfloat16)

    strip, lanes = 16, 256

    def filter_frames(first, last, row_first, row_last):
        def column(index, carry):
            start = pl.multiple_of(index * lanes, lanes)
            weights = [window_ref[tap : tap + 1, pl.ds(start, lanes)] for tap in range(TAPS)]

            def samples(place, frame):
                return extended[place, pl.ds(frame * L + start, lanes)].astype(jnp.float32)

            def one_strip(row, carry):
                place = pl.ds(pl.multiple_of(row * strip, strip), strip)
                held = [samples(place, first + tap) for tap in range(TAPS - 1)]
                for frame in range(first, last):
                    held.append(samples(place, frame + TAPS - 1))
                    value = held[0] * weights[0]
                    for tap in range(1, TAPS):
                        value = value + held[tap] * weights[tap]
                    to = pl.ds(pl.multiple_of(frame * width + row * strip, strip), strip)
                    filtered[to, pl.ds(start, lanes)] = value.astype(jnp.bfloat16)
                    held = held[1:]
                return carry

            lax.fori_loop(row_first, row_last, one_strip, jnp.int32(0))
            return carry

        lax.fori_loop(0, L // lanes, column, jnp.int32(0))

    dot_rows = min(256, group_rows)

    def transform(mask, first, last):
        start = flipped(group, mask, groups) * group_rows

        def one(pair, carry):
            taken = pl.ds(pl.multiple_of(pair * PAIR * width, PAIR * width), PAIR * width)
            for row in range(0, group_rows, dot_rows):
                place = pl.ds(pl.multiple_of(start + row, dot_rows), dot_rows)
                product = lax.dot_general(
                    table[place, :],
                    filtered[taken, :],
                    (((1,), (1,)), ((), ())),
                    preferred_element_type=jnp.float32,
                )
                for inner in range(PAIR):
                    base = (mask * group_rows + row) * frames + pair * PAIR + inner
                    where = pl.ds(base, dot_rows, stride=frames)
                    total[where, :] = product[:, inner * width : (inner + 1) * width]
            return carry

        lax.fori_loop(first, last, one, jnp.int32(0))

    def put(mask):
        first = flipped(group, mask, groups) * channels
        some = 8

        def one(index, carry):
            taken = pl.ds(
                pl.multiple_of((mask * channels + index * some) * depth, some * depth), some * depth
            )
            own[pl.ds(first + index * some, some)] = (
                total[taken, :].reshape(some, depth, width).astype(jnp.bfloat16)
            )
            return carry

        lax.fori_loop(0, channels // some, one, jnp.int32(0))

    def where(chunk):
        if isinstance(chunk, int) and chunk < 2:
            return 0, chunk * crossed, (kept - crossed if chunk else crossed)
        return 1 + (chunk - 2) // PARTS, (chunk - 2) % PARTS * step, step

    def rows_of(block, first, count, time):
        return all_ref.at[
            block, pl.ds(first, count), pl.ds(pl.multiple_of(time * depth, depth), depth)
        ]

    def part(block, chunk):
        mask, first, count = where(chunk)
        return rows_of(block, first, count, flipped(group, mask, groups))

    def own_part(chunk):
        mask, first, count = where(chunk)
        return own.at[pl.ds(flipped(group, mask, groups) * channels + first, count)]

    def turn(chunk, arriving=False):
        mask, first, count = where(chunk)
        return pltpu.make_async_remote_copy(
            src_ref=own_part(chunk),
            dst_ref=part(me, chunk) if arriving else rows_of(me, first, count, group),
            send_sem=turn_send.at[chunk],
            recv_sem=turn_recv.at[chunk],
            device_id={"chan": flipped(group, mask, groups)},
            device_id_type=MESH,
        )

    def copy(block, chunk, way, to_sems, source=None):
        place = part(block, chunk)
        return pltpu.make_async_remote_copy(
            src_ref=place if source is None else source,
            dst_ref=place,
            send_sem=to_sems.at[way[1], block],
            recv_sem=recv_sem.at[block, chunk],
            device_id={"inp": way[3]},
            device_id_type=MESH,
        )

    def send(block, chunk, ways, to_sems, source=None):
        for way in ways:

            @pl.when(way[2])
            def _(way=way):
                copy(block, chunk, way, to_sems, source).start()

    def pass_on(block, chunk, exists, ways, to_sems, origin):
        @pl.when(exists)
        def _():
            copy(block, chunk, origin, to_sems).wait_recv()
            send(block, chunk, ways, to_sems)

    def over(first, last, body):
        def one(chunk, carry):
            body(chunk)
            return carry

        for chunk in range(first, min(last, 2)):
            body(chunk)
        if last > 2:
            lax.fori_loop(max(first, 2), last, one, jnp.int32(0))

    def of_mask(mask):
        return (1, 2) if mask == 0 else (2 + (mask - 1) * PARTS, 2 + mask * PARTS)

    class Tail:
        def __init__(self, ref, first, count, index_of, ways, sems):
            self.ref, self.first, self.count, self.index_of = ref, first, count, index_of
            self.ways = ways
            self.send_sem, self.recv_sem, self.turn_send, self.turn_recv = sems

        def source(self, mask):
            return own.at[pl.ds(flipped(group, mask, groups) * channels + self.first, self.count)]

        def at(self, block, time):
            span = pl.ds(pl.multiple_of(time * depth, depth), depth)
            return self.ref.at[self.index_of(block), :, span]

        def turn(self, mask, arriving=False):
            other = flipped(group, mask, groups)
            return pltpu.make_async_remote_copy(
                src_ref=self.source(mask),
                dst_ref=self.at(me, other if arriving else group),
                send_sem=self.turn_send.at[mask],
                recv_sem=self.turn_recv.at[mask],
                device_id={"chan": other},
                device_id_type=MESH,
            )

        def copy(self, block, mask, way, source=None):
            place = self.at(block, flipped(group, mask, groups))
            return pltpu.make_async_remote_copy(
                src_ref=place if source is None else source,
                dst_ref=place,
                send_sem=self.send_sem.at[way[1], self.index_of(block)],
                recv_sem=self.recv_sem.at[self.index_of(block), mask],
                device_id={"inp": way[3]},
                device_id_type=MESH,
            )

        def send(self, block, mask, ways, source=None):
            for way in ways:

                @pl.when(way[2])
                def _(way=way):
                    self.copy(block, mask, way, source).start()

        def pass_on(self, block, mask, exists, ways, origin):
            @pl.when(exists)
            def _():
                self.copy(block, mask, origin).wait_recv()
                self.send(block, mask, ways)

        def drain(self, block, way, cond):
            @pl.when(jnp.logical_and(cond, way[2]))
            def _():
                whole = self.ref.at[self.index_of(block)]
                pltpu.make_async_remote_copy(
                    src_ref=whole,
                    dst_ref=whole,
                    send_sem=self.send_sem.at[way[1], self.index_of(block)],
                    recv_sem=self.recv_sem.at[self.index_of(block), 0],
                    device_id={"inp": way[3]},
                    device_id_type=MESH,
                ).wait_send()

    deferred, line_late, cross_late = [], None, None
    if tails:
        line_late = Tail(line_ref, kept, line_tail, lambda b: b // columns, along_z, tail_sems[:4])
        cross_late = Tail(
            cross_ref, kept + line_tail, cross_tail, lambda b: b, along_x + inner_z, tail_sems[4:]
        )
        deferred = [line_late, cross_late]

    stores = [
        pltpu.make_async_copy(
            own.at[pl.ds(group * channels, kept)],
            all_ref.at[me, :, pl.ds(pl.multiple_of(group * depth, depth), depth)],
            local_sem.at[0],
        )
    ]
    for number, tail in enumerate(deferred):
        stores.append(
            pltpu.make_async_copy(tail.source(0), tail.at(me, group), local_sem.at[1 + number])
        )

    def launch(mask):
        if mask:
            over(*of_mask(mask), lambda c: turn(c).start())
            for tail in deferred:
                tail.turn(mask).start()
        else:
            send(me, 0, along_x + along_z, send_cross, own_part(0))
            send(me, 1, along_z + along_x, send_line, own_part(1))
            for tail in deferred:
                tail.send(me, 0, tail.ways, tail.source(0))
            for store in stores:
                store.start()

    clear = max(0, (frames - TAPS + 1) // PAIR)
    early = min(2, groups)

    def loaded(index, carry):
        load(index).wait()
        many = part_rows // strip
        filter_frames(0, clear * PAIR, index * many, (index + 1) * many)
        return carry

    lax.fori_loop(0, LOADS, loaded, jnp.int32(0))
    for mask in range(early):
        load_rows(mask).wait()
        transform(mask, 0, clear)

    @pl.when(has_next)
    def _():
        halo.wait_recv()

    filter_frames(clear * PAIR, frames, 0, width // strip)
    for mask in range(groups):
        if mask >= early:
            load_rows(mask).wait()
        transform(mask, clear if mask < early else 0, frames // PAIR)
        put(mask)
        launch(mask)

    def own_turned(mask):
        def one(chunk):
            turn(chunk, True).wait_recv()
            send(me, chunk, along_z + along_x, send_line)

        over(*of_mask(mask), one)
        for tail in deferred:
            tail.turn(mask, True).wait_recv()
            tail.send(me, mask, tail.ways)

    def late(away, mask):
        if not tails:
            return
        below, above = z >= away, z + away < rows
        line_late.pass_on(me - away * columns, mask, below, (up,), down)
        line_late.pass_on(me + away * columns, mask, above, (down,), up)
        if away == 1:
            cross_late.pass_on(me - 1, mask, x >= 1, inner_z, left)
            cross_late.pass_on(me + 1, mask, x + 1 < columns, inner_z, right)
        below = jnp.logical_and(below, z < rows - 1)
        above = jnp.logical_and(above, z > 0)
        for column in range(columns):
            low = (z - away) * columns + column
            high = (z + away) * columns + column
            cross_late.pass_on(low, mask, below, inner_z[:1], down)
            cross_late.pass_on(high, mask, above, inner_z[1:], up)

    def line(away, first, last):
        below, above = z >= away, z + away < rows

        def one(chunk):
            low, high = along_x + (up,), along_x + (down,)
            if tails and away == 1:
                low, high = cut_x(z == 1) + (up,), cut_x(z == rows - 2) + (down,)
            pass_on(me - away * columns, chunk, below, low, send_line, down)
            pass_on(me + away * columns, chunk, above, high, send_line, up)

        over(first, last, one)

    def cut_x(skip):
        return tuple((n, i, jnp.logical_and(e, jnp.logical_not(skip)), t) for n, i, e, t in along_x)

    def beside(mask):
        if not tails:
            return

        def one(chunk):
            pass_on(me - 1, chunk, jnp.logical_and(at_end, x >= 1), along_z, send_line, left)
            pass_on(
                me + 1, chunk, jnp.logical_and(at_end, x + 1 < columns), along_z, send_line, right
            )

        over(*of_mask(mask), one)

    def crossing(away):
        below, above = z >= away, z + away < rows
        for column in range(columns):
            low = (z - away) * columns + column
            high = (z + away) * columns + column
            pass_on(low, 0, below, (up,), send_cross, down)
            pass_on(high, 0, above, (down,), send_cross, up)

    for away in range(1, columns):
        pass_on(me - away, 0, x >= away, (right,) + along_z, send_cross, left)
        pass_on(me + away, 0, x + away < columns, (left,) + along_z, send_cross, right)
    own_turned(1)
    beside(0)
    crossing(1)
    line(1, *of_mask(0))
    late(1, 0)
    for mask in range(2, groups):
        own_turned(mask)
        beside(mask - 1)
        line(1, *of_mask(mask - 1))
        late(1, mask - 1)
    beside(groups - 1)
    line(1, *of_mask(groups - 1))
    late(1, groups - 1)
    for away in range(2, rows):
        line(away, 1, chunks)
        crossing(away)
        for mask in range(groups):
            late(away, mask)
    for store in stores:
        store.wait()
    outward, sends_out = None, jnp.logical_or(z == 1, z == rows - 2)
    if tails:
        outward = pltpu.make_async_copy(
            cross_ref.at[pl.ds(jnp.where(z == 1, columns, 0), (rows - 1) * columns)],
            outward_ref,
            local_sem.at[3],
        )

        @pl.when(sends_out)
        def _():
            outward.start()

    for away in range(1, columns):
        for row in range(rows):
            before = row * columns + x - away
            after = row * columns + x + away
            due = jnp.logical_not(jnp.logical_and(at_end, z == row)) if tails else True

            def across(chunk):
                pass_on(before, chunk, jnp.logical_and(due, x >= away), (right,), send_line, left)
                pass_on(
                    after, chunk, jnp.logical_and(due, x + away < columns), (left,), send_line, right
                )

            over(1, chunks, across)

    def drain(block, way, cond, to_sems, count):
        @pl.when(jnp.logical_and(cond, way[2]))
        def _():
            whole = all_ref.at[block, pl.ds(0, count)]
            pltpu.make_async_remote_copy(
                src_ref=whole,
                dst_ref=whole,
                send_sem=to_sems.at[way[1], block],
                recv_sem=recv_sem.at[block, 0],
                device_id={"inp": way[3]},
                device_id_type=MESH,
            ).wait_send()

    for row in range(rows):
        for column in range(columns):
            block = row * columns + column
            here, same = x == column, z == row
            carried, over_x = here, True
            if tails:
                carried = jnp.logical_or(here, jnp.logical_and(at_end, same))
                over_x = jnp.logical_and(here, z != {0: 1, rows - 1: rows - 2}.get(row, rows))
            drain(block, up, jnp.logical_and(carried, z >= row), send_line, kept - crossed // groups)
            drain(block, down, jnp.logical_and(carried, z <= row), send_line, kept - crossed // groups)
            across_x = jnp.logical_and(over_x, x >= column)
            drain(block, right, across_x, send_line, kept - crossed // groups)
            across_x = jnp.logical_and(over_x, x <= column)
            drain(block, left, across_x, send_line, kept - crossed // groups)
            drain(block, up, z >= row, send_cross, crossed // groups)
            drain(block, down, z <= row, send_cross, crossed // groups)
            drain(block, right, jnp.logical_and(same, x >= column), send_cross, crossed // groups)
            drain(block, left, jnp.logical_and(same, x <= column), send_cross, crossed // groups)
            if tails:
                if column == 0:
                    own_column = row * columns + x
                    line_late.drain(own_column, up, z >= row)
                    line_late.drain(own_column, down, z <= row)
                cross_late.drain(block, inner_z[0], z >= row)
                cross_late.drain(block, inner_z[1], z <= row)
                cross_late.drain(block, right, jnp.logical_and(same, x >= column))
                cross_late.drain(block, left, jnp.logical_and(same, x <= column))
    over(2, chunks, lambda c: turn(c).wait_send())
    for tail in deferred:
        for mask in range(1, groups):
            tail.turn(mask).wait_send()
    if tails:

        @pl.when(sends_out)
        def _():
            outward.wait()

    @pl.when(has_last)
    def _():
        halo.wait_send()


def grid_of(devices):
    columns = 1 << (int(math.log2(devices)) // 2)
    return devices // columns, columns


def tails_of(devices, channels):
    rows, columns = grid_of(devices)
    if columns != 2 or rows < 4 or channels % 32:
        return 0, 0
    return channels * 3 // 32, channels // 16


def gathered_spectra(voltages):
    width, local_len = voltages.shape
    frames = local_len // L
    devices, groups = lax.axis_size("inp"), lax.axis_size("chan")
    rows, columns = grid_of(devices)
    channels, depth = NCH // groups, 2 * frames
    chunks = 2 + (groups - 1) * PARTS
    line_tail, cross_tail = tails_of(devices, channels)
    kept = channels - line_tail - cross_tail
    share = ((columns - 1) * rows - rows + 1) / (2 * (rows - 1) * (columns - 1))
    crossed = int((0.94 * share - cross_tail / channels) * groups * channels)
    crossed = min(crossed, kept - 16) // 16 * 16
    in_hbm = pl.BlockSpec(memory_space=pl.ANY)

    def blocks(count, some):
        return jax.ShapeDtypeStruct((count, some, groups * depth, width), jnp.bfloat16)

    out_shape, tail_sems = [blocks(devices, kept)], []
    if line_tail:
        out_shape.append(blocks(rows, line_tail))
        out_shape += [blocks(count, cross_tail) for count in (devices, devices - columns)]
        for ways, count in ((2, rows), (4, devices)):
            tail_sems += [
                pltpu.SemaphoreType.DMA((ways, count)),
                pltpu.SemaphoreType.DMA((count, groups)),
                pltpu.SemaphoreType.DMA((groups,)),
                pltpu.SemaphoreType.DMA((groups,)),
            ]
    return pl.pallas_call(
        functools.partial(
            spectra_kernel, (rows, columns, groups, crossed, line_tail, cross_tail)
        ),
        out_shape=out_shape,
        in_specs=[in_hbm, in_hbm, pl.BlockSpec(memory_space=pltpu.VMEM)],
        out_specs=[in_hbm] * len(out_shape),
        scratch_shapes=[
            pltpu.VMEM((width, local_len + (TAPS - 1) * L), jnp.bfloat16),
            pltpu.VMEM((frames * width, L), jnp.bfloat16),
            pltpu.VMEM((2 * NCH, L), jnp.bfloat16),
            pltpu.VMEM((2 * NCH * frames, width), jnp.float32),
            pltpu.VMEM((NCH, depth, width), jnp.bfloat16),
            pltpu.SemaphoreType.DMA((LOADS,)),
            pltpu.SemaphoreType.DMA((groups,)),
            pltpu.SemaphoreType.DMA((2,)),
            pltpu.SemaphoreType.DMA((4,)),
            pltpu.SemaphoreType.DMA((4, devices)),
            pltpu.SemaphoreType.DMA((4, devices)),
            pltpu.SemaphoreType.DMA((devices, chunks)),
            pltpu.SemaphoreType.DMA((chunks,)),
            pltpu.SemaphoreType.DMA((chunks,)),
            *tail_sems,
        ],
        compiler_params=pltpu.CompilerParams(
            collective_id=0, has_side_effects=True, vmem_limit_bytes=52 << 20
        ),
        name="spectra",
    )(voltages, jnp.asarray(transform_rows()), jnp.asarray(filter_window()))


def one_source(place_ref, refs, block, channel):
    return refs[0][block, channel]


def by_column(place_ref, refs, block, channel):
    row, columns = block // place_ref[3], place_ref[3]
    mine = block - row * columns == place_ref[1]
    return jnp.where(mine, refs[0][row, channel], refs[1][row, channel])


def by_row(place_ref, refs, block, channel):
    index = block - place_ref[2]
    away = jnp.logical_and(index >= 0, index < place_ref[4])
    sent = refs[1][jnp.clip(index, 0, refs[1].shape[0] - 1), channel]
    return jnp.where(away, sent, refs[0][block, channel])


def tile_kernel(fetch, count, slots, frames, groups, table_ref, place_ref, *refs):
    out_ref = refs[-1]
    depth = refs[0].shape[2]
    local = depth // (2 * groups)

    def scaled(block, channel):
        rows = fetch(place_ref, refs[:count], block, channel).astype(jnp.float32)
        autopower = jnp.sum(rows * rows, axis=0, keepdims=True) / frames + 1e-06
        return rows * (1.0 / (math.sqrt(frames) * jnp.sqrt(autopower)))

    def one(channel, carry):
        for slot in range(slots):
            first, second = table_ref[slot, 0], table_ref[slot, 1]
            left = scaled(jnp.maximum(first, 0), channel)
            left = jnp.where(first >= 0, left, jnp.zeros_like(left)).astype(jnp.bfloat16)
            right = scaled(jnp.maximum(second, 0), channel).astype(jnp.bfloat16)
            pieces = []
            for start in range(0, depth, 2 * local):
                pieces.append(-right[start + local : start + 2 * local])
                pieces.append(right[start : start + local])
            partner = jnp.concatenate([right, jnp.concatenate(pieces, axis=0)], axis=1)
            out_ref[channel, slot] = lax.dot_general(
                left, partner, (((0,), (0,)), ((), ())), preferred_element_type=jnp.float32
            )
        return carry

    lax.fori_loop(0, out_ref.shape[0], one, jnp.int32(0), unroll=2)


def make_tiles(fetch, sources, slot_rows, place, channels, first, tiles=None):
    some, depth, width = sources[0].shape[1:]
    slots = slot_rows.shape[0]
    lanes = max(width, 128)
    held = sum(source.shape[0] for source in sources)
    block_bytes = 2 * held * depth * lanes + 4 * slots * width * max(2 * width, 128)
    group = 16
    while 2 * group * block_bytes > 32 << 20 or some % group or first % group:
        group -= 1
    if tiles is not None:
        group = math.gcd(4, group)
    offset = first // group
    return pl.pallas_call(
        functools.partial(
            tile_kernel, fetch, len(sources), slots, depth // 2, lax.axis_size("chan")
        ),
        out_shape=jax.ShapeDtypeStruct((channels, slots, width, 2 * width), jnp.float32),
        grid_spec=pltpu.PrefetchScalarGridSpec(
            num_scalar_prefetch=2,
            grid=(some // group,),
            in_specs=[
                pl.BlockSpec((source.shape[0], group, depth, width), lambda c, t, p: (0, c, 0, 0))
                for source in sources
            ]
            + [pl.BlockSpec(memory_space=pl.ANY)] * (tiles is not None),
            out_specs=pl.BlockSpec(
                (group, slots, width, 2 * width), lambda c, t, p: (offset + c, 0, 0, 0)
            ),
        ),
        input_output_aliases={} if tiles is None else {2 + len(sources): 0},
        compiler_params=pltpu.CompilerParams(vmem_limit_bytes=48 << 20),
        cost_estimate=pl.CostEstimate(
            flops=some * slots * 4 * depth * width * width,
            bytes_accessed=some * (2 * held * depth * width + 8 * slots * width * width),
            transcendentals=0,
        ),
        name="tiles",
    )(slot_rows, place, *sources, *(() if tiles is None else (tiles,)))


def on_device(voltages, tile_table):
    devices, groups = lax.axis_size("inp"), lax.axis_size("chan")
    rows, columns = grid_of(devices)
    channels = NCH // groups
    slot_total = tile_table.shape[0] // devices
    me = lax.axis_index("inp")
    slot_rows = lax.dynamic_slice_in_dim(tile_table, me * slot_total, slot_total, 0)
    z, x = me // columns, me % columns
    at_end = jnp.logical_or(z == 0, z == rows - 1)
    shift = jnp.where(z == 0, columns, 0)
    sent = (rows - 1) * columns
    place = jnp.stack([z, x, shift, jnp.int32(columns), jnp.where(at_end, sent, 0)])
    place = place.astype(jnp.int32)
    main, *late = gathered_spectra(voltages)
    if not late:
        return make_tiles(one_source, [main], slot_rows, place, channels, 0)
    by_line, by_cross, outward = late
    over_x = [(i, i // columns * columns + columns - 1 - i % columns) for i in range(devices)]
    to_ends = []
    for column in range(columns):
        to_ends.append((columns + column, column))
        to_ends.append(((rows - 2) * columns + column, (rows - 1) * columns + column))
    line_other = lax.ppermute(by_line, "inp", over_x)
    cross_other = lax.ppermute(outward, "inp", to_ends)
    kept = main.shape[1]
    tiles = make_tiles(one_source, [main], slot_rows, place, channels, 0)
    tiles = make_tiles(by_column, [by_line, line_other], slot_rows, place, channels, kept, tiles)
    first = kept + by_line.shape[1]
    return make_tiles(by_row, [by_cross, cross_other], slot_rows, place, channels, first, tiles)


def solution(mesh):
    placed = (P("inp", "chan"), P())
    return jax.shard_map(
        on_device,
        mesh=mesh,
        in_specs=placed,
        out_specs=P("chan", "inp", None, None),
        check_vma=False,
    )
```

```python
import functools
import math

import jax
import jax.numpy as jnp
import ml_dtypes
import numpy as np
from jax import lax
from jax.experimental import pallas as pl
from jax.experimental.pallas import tpu as pltpu
from jax.sharding import PartitionSpec as P

L = 2048
NCH = 512
TAPS = 4
PAIR = 2
PARTS = 2
LOADS = 4
MESH = pl.DeviceIdType.MESH


def filter_window():
    positions = np.arange(TAPS * L, dtype=np.float64)
    shape_sinc = np.sinc((positions - TAPS * L / 2.0) / L)
    tapering = 0.5 - 0.5 * np.cos(2.0 * math.pi * positions / (TAPS * L))
    return (shape_sinc * tapering).reshape(TAPS, L).astype(np.float32)


def transform_rows():
    channels, samples = np.arange(NCH)[:, None], np.arange(L)[None, :]
    angles = (channels * samples % L) * (2.0 * math.pi / L)
    both = np.stack([np.cos(angles), -np.sin(angles)], axis=1)
    return both.reshape(2 * NCH, L).astype(ml_dtypes.bfloat16)


def flipped(group, mask, groups):
    result, bit = group, 1
    while bit < groups:
        result = result + (mask // bit % 2) * bit * (1 - 2 * (group // bit % 2))
        bit *= 2
    return result


def spectra_kernel(sizes, volt_ref, rows_ref, window_ref, all_ref, *scratch):
    rows, columns, groups, crossed, line_tail, cross_tail = sizes
    tails = line_tail + cross_tail
    if tails:
        line_ref, cross_ref, outward_ref, *scratch = scratch
    extended, filtered, table, total, own = scratch[:5]
    load_sem, table_sem, halo_sem, local_sem = scratch[5:9]
    send_line, send_cross, recv_sem, turn_send, turn_recv = scratch[9:14]
    tail_sems = scratch[14:]
    width, local_len = volt_ref.shape
    frames = local_len // L
    halo_len = (TAPS - 1) * L
    channels, depth = own.shape[0] // groups, own.shape[1]
    group_rows = 2 * channels
    kept = channels - tails
    step = kept // PARTS
    chunks = 2 + (groups - 1) * PARTS
    me, group = lax.axis_index("inp"), lax.axis_index("chan")
    has_next, has_last = group < groups - 1, group > 0
    z, x = me // columns, me % columns
    up = ("up", 0, z < rows - 1, me + columns)
    down = ("down", 1, z > 0, me - columns)
    right = ("right", 2, x < columns - 1, me + 1)
    left = ("left", 3, x > 0, me - 1)
    along_z, along_x = (up, down), (right, left)
    at_end = jnp.logical_or(z == 0, z == rows - 1)
    inner_z = (("up", 0, z < rows - 2, me + columns), ("down", 1, z > 1, me - columns))
    part_rows = width // LOADS

    def load(index):
        place = pl.ds(pl.multiple_of(index * part_rows, part_rows), part_rows)
        return pltpu.make_async_copy(
            volt_ref.at[place], extended.at[place, pl.ds(0, local_len)], load_sem.at[index]
        )

    def load_rows(mask):
        first = pl.multiple_of(flipped(group, mask, groups) * group_rows, group_rows)
        place = pl.ds(first, group_rows)
        return pltpu.make_async_copy(rows_ref.at[place], table.at[place], table_sem.at[mask])

    for index in range(LOADS):
        load(index).start()
    for mask in range(groups):
        load_rows(mask).start()

    barrier = pltpu.get_barrier_semaphore()
    expected = jnp.int32(groups - 1)
    for mask in range(1, groups):
        target = flipped(group, mask, groups)
        pl.semaphore_signal(barrier, inc=1, device_id={"chan": target}, device_id_type=MESH)
    for _, _, exists, target in along_z + along_x:
        expected = expected + exists.astype(jnp.int32)

        @pl.when(exists)
        def _(target=target):
            pl.semaphore_signal(barrier, inc=1, device_id={"inp": target}, device_id_type=MESH)

    pl.semaphore_wait(barrier, expected)
    halo = pltpu.make_async_remote_copy(
        src_ref=volt_ref.at[:, pl.ds(0, halo_len)],
        dst_ref=extended.at[:, pl.ds(local_len, halo_len)],
        send_sem=halo_sem.at[0],
        recv_sem=halo_sem.at[1],
        device_id={"chan": group - 1},
        device_id_type=MESH,
    )

    @pl.when(has_last)
    def _():
        halo.start()

    @pl.when(jnp.logical_not(has_next))
    def _():
        extended[:, pl.ds(local_len, halo_len)] = jnp.zeros((width, halo_len), jnp.bfloat16)

    strip, lanes = 16, 256

    def filter_frames(first, last, row_first, row_last):
        def column(index, carry):
            start = pl.multiple_of(index * lanes, lanes)
            weights = [window_ref[tap : tap + 1, pl.ds(start, lanes)] for tap in range(TAPS)]

            def samples(place, frame):
                return extended[place, pl.ds(frame * L + start, lanes)].astype(jnp.float32)

            def one_strip(row, carry):
                place = pl.ds(pl.multiple_of(row * strip, strip), strip)
                held = [samples(place, first + tap) for tap in range(TAPS - 1)]
                for frame in range(first, last):
                    held.append(samples(place, frame + TAPS - 1))
                    value = held[0] * weights[0]
                    for tap in range(1, TAPS):
                        value = value + held[tap] * weights[tap]
                    to = pl.ds(pl.multiple_of(frame * width + row * strip, strip), strip)
                    filtered[to, pl.ds(start, lanes)] = value.astype(jnp.bfloat16)
                    held = held[1:]
                return carry

            lax.fori_loop(row_first, row_last, one_strip, jnp.int32(0))
            return carry

        lax.fori_loop(0, L // lanes, column, jnp.int32(0))

    dot_rows = min(256, group_rows)

    def transform(mask, first, last):
        start = flipped(group, mask, groups) * group_rows

        def one(pair, carry):
            taken = pl.ds(pl.multiple_of(pair * PAIR * width, PAIR * width), PAIR * width)
            for row in range(0, group_rows, dot_rows):
                place = pl.ds(pl.multiple_of(start + row, dot_rows), dot_rows)
                product = lax.dot_general(
                    table[place, :],
                    filtered[taken, :],
                    (((1,), (1,)), ((), ())),
                    preferred_element_type=jnp.float32,
                )
                for inner in range(PAIR):
                    base = (mask * group_rows + row) * frames + pair * PAIR + inner
                    where = pl.ds(base, dot_rows, stride=frames)
                    total[where, :] = product[:, inner * width : (inner + 1) * width]
            return carry

        lax.fori_loop(first, last, one, jnp.int32(0))

    def put(mask):
        first = flipped(group, mask, groups) * channels
        some = 8

        def one(index, carry):
            taken = pl.ds(
                pl.multiple_of((mask * channels + index * some) * depth, some * depth), some * depth
            )
            own[pl.ds(first + index * some, some)] = (
                total[taken, :].reshape(some, depth, width).astype(jnp.bfloat16)
            )
            return carry

        lax.fori_loop(0, channels // some, one, jnp.int32(0))

    def where(chunk):
        if isinstance(chunk, int) and chunk < 2:
            return 0, chunk * crossed, (kept - crossed if chunk else crossed)
        return 1 + (chunk - 2) // PARTS, (chunk - 2) % PARTS * step, step

    def rows_of(block, first, count, time):
        return all_ref.at[
            block, pl.ds(first, count), pl.ds(pl.multiple_of(time * depth, depth), depth)
        ]

    def part(block, chunk):
        mask, first, count = where(chunk)
        return rows_of(block, first, count, flipped(group, mask, groups))

    def own_part(chunk):
        mask, first, count = where(chunk)
        return own.at[pl.ds(flipped(group, mask, groups) * channels + first, count)]

    def turn(chunk, arriving=False):
        mask, first, count = where(chunk)
        return pltpu.make_async_remote_copy(
            src_ref=own_part(chunk),
            dst_ref=part(me, chunk) if arriving else rows_of(me, first, count, group),
            send_sem=turn_send.at[chunk],
            recv_sem=turn_recv.at[chunk],
            device_id={"chan": flipped(group, mask, groups)},
            device_id_type=MESH,
        )

    def copy(block, chunk, way, to_sems, source=None):
        place = part(block, chunk)
        return pltpu.make_async_remote_copy(
            src_ref=place if source is None else source,
            dst_ref=place,
            send_sem=to_sems.at[way[1], block],
            recv_sem=recv_sem.at[block, chunk],
            device_id={"inp": way[3]},
            device_id_type=MESH,
        )

    def send(block, chunk, ways, to_sems, source=None):
        for way in ways:

            @pl.when(way[2])
            def _(way=way):
                copy(block, chunk, way, to_sems, source).start()

    def pass_on(block, chunk, exists, ways, to_sems, origin):
        @pl.when(exists)
        def _():
            copy(block, chunk, origin, to_sems).wait_recv()
            send(block, chunk, ways, to_sems)

    def over(first, last, body):
        def one(chunk, carry):
            body(chunk)
            return carry

        for chunk in range(first, min(last, 2)):
            body(chunk)
        if last > 2:
            lax.fori_loop(max(first, 2), last, one, jnp.int32(0))

    def of_mask(mask):
        return (1, 2) if mask == 0 else (2 + (mask - 1) * PARTS, 2 + mask * PARTS)

    class Tail:
        def __init__(self, ref, first, count, index_of, ways, sems):
            self.ref, self.first, self.count, self.index_of = ref, first, count, index_of
            self.ways = ways
            self.send_sem, self.recv_sem, self.turn_send, self.turn_recv = sems

        def source(self, mask):
            return own.at[pl.ds(flipped(group, mask, groups) * channels + self.first, self.count)]

        def at(self, block, time):
            span = pl.ds(pl.multiple_of(time * depth, depth), depth)
            return self.ref.at[self.index_of(block), :, span]

        def turn(self, mask, arriving=False):
            other = flipped(group, mask, groups)
            return pltpu.make_async_remote_copy(
                src_ref=self.source(mask),
                dst_ref=self.at(me, other if arriving else group),
                send_sem=self.turn_send.at[mask],
                recv_sem=self.turn_recv.at[mask],
                device_id={"chan": other},
                device_id_type=MESH,
            )

        def copy(self, block, mask, way, source=None):
            place = self.at(block, flipped(group, mask, groups))
            return pltpu.make_async_remote_copy(
                src_ref=place if source is None else source,
                dst_ref=place,
                send_sem=self.send_sem.at[way[1], self.index_of(block)],
                recv_sem=self.recv_sem.at[self.index_of(block), mask],
                device_id={"inp": way[3]},
                device_id_type=MESH,
            )

        def send(self, block, mask, ways, source=None):
            for way in ways:

                @pl.when(way[2])
                def _(way=way):
                    self.copy(block, mask, way, source).start()

        def pass_on(self, block, mask, exists, ways, origin):
            @pl.when(exists)
            def _():
                self.copy(block, mask, origin).wait_recv()
                self.send(block, mask, ways)

        def drain(self, block, way, cond):
            @pl.when(jnp.logical_and(cond, way[2]))
            def _():
                whole = self.ref.at[self.index_of(block)]
                pltpu.make_async_remote_copy(
                    src_ref=whole,
                    dst_ref=whole,
                    send_sem=self.send_sem.at[way[1], self.index_of(block)],
                    recv_sem=self.recv_sem.at[self.index_of(block), 0],
                    device_id={"inp": way[3]},
                    device_id_type=MESH,
                ).wait_send()

    deferred, line_late, cross_late = [], None, None
    if tails:
        line_late = Tail(line_ref, kept, line_tail, lambda b: b // columns, along_z, tail_sems[:4])
        cross_late = Tail(
            cross_ref, kept + line_tail, cross_tail, lambda b: b, along_x + inner_z, tail_sems[4:]
        )
        deferred = [line_late, cross_late]

    stores = [
        pltpu.make_async_copy(
            own.at[pl.ds(group * channels, kept)],
            all_ref.at[me, :, pl.ds(pl.multiple_of(group * depth, depth), depth)],
            local_sem.at[0],
        )
    ]
    for number, tail in enumerate(deferred):
        stores.append(
            pltpu.make_async_copy(tail.source(0), tail.at(me, group), local_sem.at[1 + number])
        )

    def launch(mask):
        if mask:
            over(*of_mask(mask), lambda c: turn(c).start())
            for tail in deferred:
                tail.turn(mask).start()
        else:
            send(me, 0, along_x + along_z, send_cross, own_part(0))
            send(me, 1, along_z + along_x, send_line, own_part(1))
            for tail in deferred:
                tail.send(me, 0, tail.ways, tail.source(0))
            for store in stores:
                store.start()

    clear = max(0, (frames - TAPS + 1) // PAIR)
    late_halo = jnp.logical_and(group % 2 == 1, has_next)
    ahead = [clear] + [jnp.where(late_halo, clear, 0)] * (groups - 1)

    def loaded(index, carry):
        load(index).wait()
        many = part_rows // strip
        filter_frames(0, clear * PAIR, index * many, (index + 1) * many)
        return carry

    lax.fori_loop(0, LOADS, loaded, jnp.int32(0))
    for mask in range(groups):
        load_rows(mask).wait()
        transform(mask, 0, ahead[mask])

    @pl.when(has_next)
    def _():
        halo.wait_recv()

    filter_frames(clear * PAIR, frames, 0, width // strip)
    for mask in range(groups):
        transform(mask, ahead[mask], frames // PAIR)
        put(mask)
        launch(mask)

    def own_turned(mask):
        def one(chunk):
            turn(chunk, True).wait_recv()
            send(me, chunk, along_z + along_x, send_line)

        over(*of_mask(mask), one)
        for tail in deferred:
            tail.turn(mask, True).wait_recv()
            tail.send(me, mask, tail.ways)

    def late(away, mask):
        if not tails:
            return
        below, above = z >= away, z + away < rows
        line_late.pass_on(me - away * columns, mask, below, (up,), down)
        line_late.pass_on(me + away * columns, mask, above, (down,), up)
        if away == 1:
            cross_late.pass_on(me - 1, mask, x >= 1, inner_z, left)
            cross_late.pass_on(me + 1, mask, x + 1 < columns, inner_z, right)
        below = jnp.logical_and(below, z < rows - 1)
        above = jnp.logical_and(above, z > 0)
        for column in range(columns):
            low = (z - away) * columns + column
            high = (z + away) * columns + column
            cross_late.pass_on(low, mask, below, inner_z[:1], down)
            cross_late.pass_on(high, mask, above, inner_z[1:], up)

    def line(away, first, last):
        below, above = z >= away, z + away < rows

        def one(chunk):
            low, high = along_x + (up,), along_x + (down,)
            if tails and away == 1:
                low, high = cut_x(z == 1) + (up,), cut_x(z == rows - 2) + (down,)
            pass_on(me - away * columns, chunk, below, low, send_line, down)
            pass_on(me + away * columns, chunk, above, high, send_line, up)

        over(first, last, one)

    def cut_x(skip):
        return tuple((n, i, jnp.logical_and(e, jnp.logical_not(skip)), t) for n, i, e, t in along_x)

    def beside(mask):
        if not tails:
            return

        def one(chunk):
            pass_on(me - 1, chunk, jnp.logical_and(at_end, x >= 1), along_z, send_line, left)
            pass_on(
                me + 1, chunk, jnp.logical_and(at_end, x + 1 < columns), along_z, send_line, right
            )

        over(*of_mask(mask), one)

    def crossing(away):
        below, above = z >= away, z + away < rows
        for column in range(columns):
            low = (z - away) * columns + column
            high = (z + away) * columns + column
            pass_on(low, 0, below, (up,), send_cross, down)
            pass_on(high, 0, above, (down,), send_cross, up)

    for away in range(1, columns):
        pass_on(me - away, 0, x >= away, (right,) + along_z, send_cross, left)
        pass_on(me + away, 0, x + away < columns, (left,) + along_z, send_cross, right)
    own_turned(1)
    beside(0)
    crossing(1)
    line(1, *of_mask(0))
    late(1, 0)
    for mask in range(2, groups):
        own_turned(mask)
        beside(mask - 1)
        line(1, *of_mask(mask - 1))
        late(1, mask - 1)
    beside(groups - 1)
    line(1, *of_mask(groups - 1))
    late(1, groups - 1)
    for away in range(2, rows):
        line(away, 1, chunks)
        crossing(away)
        for mask in range(groups):
            late(away, mask)
    for store in stores:
        store.wait()
    outward, sends_out = None, jnp.logical_or(z == 1, z == rows - 2)
    if tails:
        outward = pltpu.make_async_copy(
            cross_ref.at[pl.ds(jnp.where(z == 1, columns, 0), (rows - 1) * columns)],
            outward_ref,
            local_sem.at[3],
        )

        @pl.when(sends_out)
        def _():
            outward.start()

    for away in range(1, columns):
        for row in range(rows):
            before = row * columns + x - away
            after = row * columns + x + away
            due = jnp.logical_not(jnp.logical_and(at_end, z == row)) if tails else True

            def across(chunk):
                pass_on(before, chunk, jnp.logical_and(due, x >= away), (right,), send_line, left)
                pass_on(
                    after, chunk, jnp.logical_and(due, x + away < columns), (left,), send_line, right
                )

            over(1, chunks, across)

    def drain(block, way, cond, to_sems, count):
        @pl.when(jnp.logical_and(cond, way[2]))
        def _():
            whole = all_ref.at[block, pl.ds(0, count)]
            pltpu.make_async_remote_copy(
                src_ref=whole,
                dst_ref=whole,
                send_sem=to_sems.at[way[1], block],
                recv_sem=recv_sem.at[block, 0],
                device_id={"inp": way[3]},
                device_id_type=MESH,
            ).wait_send()

    for row in range(rows):
        for column in range(columns):
            block = row * columns + column
            here, same = x == column, z == row
            carried, over_x = here, True
            if tails:
                carried = jnp.logical_or(here, jnp.logical_and(at_end, same))
                over_x = jnp.logical_and(here, z != {0: 1, rows - 1: rows - 2}.get(row, rows))
            drain(block, up, jnp.logical_and(carried, z >= row), send_line, kept - crossed // groups)
            drain(block, down, jnp.logical_and(carried, z <= row), send_line, kept - crossed // groups)
            across_x = jnp.logical_and(over_x, x >= column)
            drain(block, right, across_x, send_line, kept - crossed // groups)
            across_x = jnp.logical_and(over_x, x <= column)
            drain(block, left, across_x, send_line, kept - crossed // groups)
            drain(block, up, z >= row, send_cross, crossed // groups)
            drain(block, down, z <= row, send_cross, crossed // groups)
            drain(block, right, jnp.logical_and(same, x >= column), send_cross, crossed // groups)
            drain(block, left, jnp.logical_and(same, x <= column), send_cross, crossed // groups)
            if tails:
                if column == 0:
                    own_column = row * columns + x
                    line_late.drain(own_column, up, z >= row)
                    line_late.drain(own_column, down, z <= row)
                cross_late.drain(block, inner_z[0], z >= row)
                cross_late.drain(block, inner_z[1], z <= row)
                cross_late.drain(block, right, jnp.logical_and(same, x >= column))
                cross_late.drain(block, left, jnp.logical_and(same, x <= column))
    over(2, chunks, lambda c: turn(c).wait_send())
    for tail in deferred:
        for mask in range(1, groups):
            tail.turn(mask).wait_send()
    if tails:

        @pl.when(sends_out)
        def _():
            outward.wait()

    @pl.when(has_last)
    def _():
        halo.wait_send()


def grid_of(devices):
    columns = 1 << (int(math.log2(devices)) // 2)
    return devices // columns, columns


def tails_of(devices, channels):
    rows, columns = grid_of(devices)
    if columns != 2 or rows < 4 or channels % 32:
        return 0, 0
    return channels * 3 // 32, channels // 16


def gathered_spectra(voltages):
    width, local_len = voltages.shape
    frames = local_len // L
    devices, groups = lax.axis_size("inp"), lax.axis_size("chan")
    rows, columns = grid_of(devices)
    channels, depth = NCH // groups, 2 * frames
    chunks = 2 + (groups - 1) * PARTS
    line_tail, cross_tail = tails_of(devices, channels)
    kept = channels - line_tail - cross_tail
    share = ((columns - 1) * rows - rows + 1) / (2 * (rows - 1) * (columns - 1))
    crossed = int((0.94 * share - cross_tail / channels) * groups * channels)
    crossed = min(crossed, kept - 16) // 16 * 16
    in_hbm = pl.BlockSpec(memory_space=pl.ANY)

    def blocks(count, some):
        return jax.ShapeDtypeStruct((count, some, groups * depth, width), jnp.bfloat16)

    out_shape, tail_sems = [blocks(devices, kept)], []
    if line_tail:
        out_shape.append(blocks(rows, line_tail))
        out_shape += [blocks(count, cross_tail) for count in (devices, devices - columns)]
        for ways, count in ((2, rows), (4, devices)):
            tail_sems += [
                pltpu.SemaphoreType.DMA((ways, count)),
                pltpu.SemaphoreType.DMA((count, groups)),
                pltpu.SemaphoreType.DMA((groups,)),
                pltpu.SemaphoreType.DMA((groups,)),
            ]
    return pl.pallas_call(
        functools.partial(
            spectra_kernel, (rows, columns, groups, crossed, line_tail, cross_tail)
        ),
        out_shape=out_shape,
        in_specs=[in_hbm, in_hbm, pl.BlockSpec(memory_space=pltpu.VMEM)],
        out_specs=[in_hbm] * len(out_shape),
        scratch_shapes=[
            pltpu.VMEM((width, local_len + (TAPS - 1) * L), jnp.bfloat16),
            pltpu.VMEM((frames * width, L), jnp.bfloat16),
            pltpu.VMEM((2 * NCH, L), jnp.bfloat16),
            pltpu.VMEM((2 * NCH * frames, width), jnp.float32),
            pltpu.VMEM((NCH, depth, width), jnp.bfloat16),
            pltpu.SemaphoreType.DMA((LOADS,)),
            pltpu.SemaphoreType.DMA((groups,)),
            pltpu.SemaphoreType.DMA((2,)),
            pltpu.SemaphoreType.DMA((4,)),
            pltpu.SemaphoreType.DMA((4, devices)),
            pltpu.SemaphoreType.DMA((4, devices)),
            pltpu.SemaphoreType.DMA((devices, chunks)),
            pltpu.SemaphoreType.DMA((chunks,)),
            pltpu.SemaphoreType.DMA((chunks,)),
            *tail_sems,
        ],
        compiler_params=pltpu.CompilerParams(
            collective_id=0, has_side_effects=True, vmem_limit_bytes=52 << 20
        ),
        name="spectra",
    )(voltages, jnp.asarray(transform_rows()), jnp.asarray(filter_window()))


def one_source(place_ref, refs, block, channel):
    return refs[0][block, channel]


def by_column(place_ref, refs, block, channel):
    row, columns = block // place_ref[3], place_ref[3]
    mine = block - row * columns == place_ref[1]
    return jnp.where(mine, refs[0][row, channel], refs[1][row, channel])


def by_row(place_ref, refs, block, channel):
    index = block - place_ref[2]
    away = jnp.logical_and(index >= 0, index < place_ref[4])
    sent = refs[1][jnp.clip(index, 0, refs[1].shape[0] - 1), channel]
    return jnp.where(away, sent, refs[0][block, channel])


def tile_kernel(fetch, count, slots, frames, groups, table_ref, place_ref, *refs):
    out_ref = refs[-1]
    depth = refs[0].shape[2]
    local = depth // (2 * groups)

    def scaled(block, channel):
        rows = fetch(place_ref, refs[:count], block, channel).astype(jnp.float32)
        autopower = jnp.sum(rows * rows, axis=0, keepdims=True) / frames + 1e-06
        return rows * (1.0 / (math.sqrt(frames) * jnp.sqrt(autopower)))

    def one(channel, carry):
        for slot in range(slots):
            first, second = table_ref[slot, 0], table_ref[slot, 1]
            left = scaled(jnp.maximum(first, 0), channel)
            left = jnp.where(first >= 0, left, jnp.zeros_like(left)).astype(jnp.bfloat16)
            right = scaled(jnp.maximum(second, 0), channel).astype(jnp.bfloat16)
            pieces = []
            for start in range(0, depth, 2 * local):
                pieces.append(-right[start + local : start + 2 * local])
                pieces.append(right[start : start + local])
            partner = jnp.concatenate([right, jnp.concatenate(pieces, axis=0)], axis=1)
            out_ref[channel, slot] = lax.dot_general(
                left, partner, (((0,), (0,)), ((), ())), preferred_element_type=jnp.float32
            )
        return carry

    lax.fori_loop(0, out_ref.shape[0], one, jnp.int32(0), unroll=2)


def make_tiles(fetch, sources, slot_rows, place, channels, first, tiles=None):
    some, depth, width = sources[0].shape[1:]
    slots = slot_rows.shape[0]
    lanes = max(width, 128)
    held = sum(source.shape[0] for source in sources)
    block_bytes = 2 * held * depth * lanes + 4 * slots * width * max(2 * width, 128)
    group = 16
    while 2 * group * block_bytes > 32 << 20 or some % group or first % group:
        group -= 1
    if tiles is not None:
        group = max(1, group // 2)
    offset = first // group
    return pl.pallas_call(
        functools.partial(
            tile_kernel, fetch, len(sources), slots, depth // 2, lax.axis_size("chan")
        ),
        out_shape=jax.ShapeDtypeStruct((channels, slots, width, 2 * width), jnp.float32),
        grid_spec=pltpu.PrefetchScalarGridSpec(
            num_scalar_prefetch=2,
            grid=(some // group,),
            in_specs=[
                pl.BlockSpec((source.shape[0], group, depth, width), lambda c, t, p: (0, c, 0, 0))
                for source in sources
            ]
            + [pl.BlockSpec(memory_space=pl.ANY)] * (tiles is not None),
            out_specs=pl.BlockSpec(
                (group, slots, width, 2 * width), lambda c, t, p: (offset + c, 0, 0, 0)
            ),
        ),
        input_output_aliases={} if tiles is None else {2 + len(sources): 0},
        compiler_params=pltpu.CompilerParams(vmem_limit_bytes=48 << 20),
        cost_estimate=pl.CostEstimate(
            flops=some * slots * 4 * depth * width * width,
            bytes_accessed=some * (2 * held * depth * width + 8 * slots * width * width),
            transcendentals=0,
        ),
        name="tiles",
    )(slot_rows, place, *sources, *(() if tiles is None else (tiles,)))


def on_device(voltages, tile_table):
    devices, groups = lax.axis_size("inp"), lax.axis_size("chan")
    rows, columns = grid_of(devices)
    channels = NCH // groups
    slot_total = tile_table.shape[0] // devices
    me = lax.axis_index("inp")
    slot_rows = lax.dynamic_slice_in_dim(tile_table, me * slot_total, slot_total, 0)
    z, x = me // columns, me % columns
    at_end = jnp.logical_or(z == 0, z == rows - 1)
    shift = jnp.where(z == 0, columns, 0)
    sent = (rows - 1) * columns
    place = jnp.stack([z, x, shift, jnp.int32(columns), jnp.where(at_end, sent, 0)])
    place = place.astype(jnp.int32)
    main, *late = gathered_spectra(voltages)
    if not late:
        return make_tiles(one_source, [main], slot_rows, place, channels, 0)
    by_line, by_cross, outward = late
    over_x = [(i, i // columns * columns + columns - 1 - i % columns) for i in range(devices)]
    to_ends = []
    for column in range(columns):
        to_ends.append((columns + column, column))
        to_ends.append(((rows - 2) * columns + column, (rows - 1) * columns + column))
    line_other = lax.ppermute(by_line, "inp", over_x)
    cross_other = lax.ppermute(outward, "inp", to_ends)
    kept = main.shape[1]
    tiles = make_tiles(one_source, [main], slot_rows, place, channels, 0)
    tiles = make_tiles(by_column, [by_line, line_other], slot_rows, place, channels, kept, tiles)
    first = kept + by_line.shape[1]
    return make_tiles(by_row, [by_cross, cross_other], slot_rows, place, channels, first, tiles)


def solution(mesh):
    placed = (P("inp", "chan"), P())
    return jax.shard_map(
        on_device,
        mesh=mesh,
        in_specs=placed,
        out_specs=P("chan", "inp", None, None),
        check_vma=False,
    )
```

```python
import functools
import math

import jax
import jax.numpy as jnp
import ml_dtypes
import numpy as np
from jax import lax
from jax.experimental import pallas as pl
from jax.experimental.pallas import tpu as pltpu
from jax.sharding import PartitionSpec as P

L = 2048
NCH = 512
TAPS = 4
PAIR = 2
PARTS = 2
LOADS = 4
MESH = pl.DeviceIdType.MESH


def filter_window():
    positions = np.arange(TAPS * L, dtype=np.float64)
    shape_sinc = np.sinc((positions - TAPS * L / 2.0) / L)
    tapering = 0.5 - 0.5 * np.cos(2.0 * math.pi * positions / (TAPS * L))
    return (shape_sinc * tapering).reshape(TAPS, L).astype(np.float32)


def transform_rows():
    channels, samples = np.arange(NCH)[:, None], np.arange(L)[None, :]
    angles = (channels * samples % L) * (2.0 * math.pi / L)
    both = np.stack([np.cos(angles), -np.sin(angles)], axis=1)
    return both.reshape(2 * NCH, L).astype(ml_dtypes.bfloat16)


def flipped(group, mask, groups):
    result, bit = group, 1
    while bit < groups:
        result = result + (mask // bit % 2) * bit * (1 - 2 * (group // bit % 2))
        bit *= 2
    return result


def spectra_kernel(sizes, volt_ref, rows_ref, window_ref, all_ref, *scratch):
    rows, columns, groups, crossed, line_tail, cross_tail = sizes
    tails = line_tail + cross_tail
    if tails:
        line_ref, cross_ref, outward_ref, *scratch = scratch
    extended, filtered, table, total, own = scratch[:5]
    load_sem, table_sem, halo_sem, local_sem = scratch[5:9]
    send_line, send_cross, recv_sem, turn_send, turn_recv = scratch[9:14]
    tail_sems = scratch[14:]
    width, local_len = volt_ref.shape
    frames = local_len // L
    halo_len = (TAPS - 1) * L
    channels, depth = own.shape[0] // groups, own.shape[1]
    group_rows = 2 * channels
    kept = channels - tails
    step = kept // PARTS
    chunks = 2 + (groups - 1) * PARTS
    me, group = lax.axis_index("inp"), lax.axis_index("chan")
    has_next, has_last = group < groups - 1, group > 0
    z, x = me // columns, me % columns
    up = ("up", 0, z < rows - 1, me + columns)
    down = ("down", 1, z > 0, me - columns)
    right = ("right", 2, x < columns - 1, me + 1)
    left = ("left", 3, x > 0, me - 1)
    along_z, along_x = (up, down), (right, left)
    at_end = jnp.logical_or(z == 0, z == rows - 1)
    inner_z = (("up", 0, z < rows - 2, me + columns), ("down", 1, z > 1, me - columns))
    part_rows = width // LOADS

    def load(index):
        place = pl.ds(pl.multiple_of(index * part_rows, part_rows), part_rows)
        return pltpu.make_async_copy(
            volt_ref.at[place], extended.at[place, pl.ds(0, local_len)], load_sem.at[index]
        )

    def load_rows(mask):
        first = pl.multiple_of(flipped(group, mask, groups) * group_rows, group_rows)
        place = pl.ds(first, group_rows)
        return pltpu.make_async_copy(rows_ref.at[place], table.at[place], table_sem.at[mask])

    for index in range(LOADS):
        load(index).start()
    for mask in range(groups):
        load_rows(mask).start()

    barrier = pltpu.get_barrier_semaphore()
    expected = jnp.int32(groups - 1)
    for mask in range(1, groups):
        target = flipped(group, mask, groups)
        pl.semaphore_signal(barrier, inc=1, device_id={"chan": target}, device_id_type=MESH)
    for _, _, exists, target in along_z + along_x:
        expected = expected + exists.astype(jnp.int32)

        @pl.when(exists)
        def _(target=target):
            pl.semaphore_signal(barrier, inc=1, device_id={"inp": target}, device_id_type=MESH)

    pl.semaphore_wait(barrier, expected)
    halo = pltpu.make_async_remote_copy(
        src_ref=volt_ref.at[:, pl.ds(0, halo_len)],
        dst_ref=extended.at[:, pl.ds(local_len, halo_len)],
        send_sem=halo_sem.at[0],
        recv_sem=halo_sem.at[1],
        device_id={"chan": group - 1},
        device_id_type=MESH,
    )

    @pl.when(has_last)
    def _():
        halo.start()

    @pl.when(jnp.logical_not(has_next))
    def _():
        extended[:, pl.ds(local_len, halo_len)] = jnp.zeros((width, halo_len), jnp.bfloat16)

    strip, lanes = 16, 256

    def filter_frames(first, last, row_first, row_last):
        def column(index, carry):
            start = pl.multiple_of(index * lanes, lanes)
            weights = [window_ref[tap : tap + 1, pl.ds(start, lanes)] for tap in range(TAPS)]

            def samples(place, frame):
                return extended[place, pl.ds(frame * L + start, lanes)].astype(jnp.float32)

            def one_strip(row, carry):
                place = pl.ds(pl.multiple_of(row * strip, strip), strip)
                held = [samples(place, first + tap) for tap in range(TAPS - 1)]
                for frame in range(first, last):
                    held.append(samples(place, frame + TAPS - 1))
                    value = held[0] * weights[0]
                    for tap in range(1, TAPS):
                        value = value + held[tap] * weights[tap]
                    to = pl.ds(pl.multiple_of(frame * width + row * strip, strip), strip)
                    filtered[to, pl.ds(start, lanes)] = value.astype(jnp.bfloat16)
                    held = held[1:]
                return carry

            lax.fori_loop(row_first, row_last, one_strip, jnp.int32(0))
            return carry

        lax.fori_loop(0, L // lanes, column, jnp.int32(0))

    dot_rows = min(256, group_rows)

    def transform(mask, first, last):
        start = flipped(group, mask, groups) * group_rows

        def one(pair, carry):
            taken = pl.ds(pl.multiple_of(pair * PAIR * width, PAIR * width), PAIR * width)
            for row in range(0, group_rows, dot_rows):
                place = pl.ds(pl.multiple_of(start + row, dot_rows), dot_rows)
                product = lax.dot_general(
                    table[place, :],
                    filtered[taken, :],
                    (((1,), (1,)), ((), ())),
                    preferred_element_type=jnp.float32,
                )
                for inner in range(PAIR):
                    base = (mask * group_rows + row) * frames + pair * PAIR + inner
                    where = pl.ds(base, dot_rows, stride=frames)
                    total[where, :] = product[:, inner * width : (inner + 1) * width]
            return carry

        lax.fori_loop(first, last, one, jnp.int32(0))

    def put(mask):
        first = flipped(group, mask, groups) * channels
        some = 8

        def one(index, carry):
            taken = pl.ds(
                pl.multiple_of((mask * channels + index * some) * depth, some * depth), some * depth
            )
            own[pl.ds(first + index * some, some)] = (
                total[taken, :].reshape(some, depth, width).astype(jnp.bfloat16)
            )
            return carry

        lax.fori_loop(0, channels // some, one, jnp.int32(0))

    def where(chunk):
        if isinstance(chunk, int) and chunk < 2:
            return 0, chunk * crossed, (kept - crossed if chunk else crossed)
        return 1 + (chunk - 2) // PARTS, (chunk - 2) % PARTS * step, step

    def rows_of(block, first, count, time):
        return all_ref.at[
            block, pl.ds(first, count), pl.ds(pl.multiple_of(time * depth, depth), depth)
        ]

    def part(block, chunk):
        mask, first, count = where(chunk)
        return rows_of(block, first, count, flipped(group, mask, groups))

    def own_part(chunk):
        mask, first, count = where(chunk)
        return own.at[pl.ds(flipped(group, mask, groups) * channels + first, count)]

    def turn(chunk, arriving=False):
        mask, first, count = where(chunk)
        return pltpu.make_async_remote_copy(
            src_ref=own_part(chunk),
            dst_ref=part(me, chunk) if arriving else rows_of(me, first, count, group),
            send_sem=turn_send.at[chunk],
            recv_sem=turn_recv.at[chunk],
            device_id={"chan": flipped(group, mask, groups)},
            device_id_type=MESH,
        )

    def copy(block, chunk, way, to_sems, source=None):
        place = part(block, chunk)
        return pltpu.make_async_remote_copy(
            src_ref=place if source is None else source,
            dst_ref=place,
            send_sem=to_sems.at[way[1], block],
            recv_sem=recv_sem.at[block, chunk],
            device_id={"inp": way[3]},
            device_id_type=MESH,
        )

    def send(block, chunk, ways, to_sems, source=None):
        for way in ways:

            @pl.when(way[2])
            def _(way=way):
                copy(block, chunk, way, to_sems, source).start()

    def pass_on(block, chunk, exists, ways, to_sems, origin):
        @pl.when(exists)
        def _():
            copy(block, chunk, origin, to_sems).wait_recv()
            send(block, chunk, ways, to_sems)

    def over(first, last, body):
        def one(chunk, carry):
            body(chunk)
            return carry

        for chunk in range(first, min(last, 2)):
            body(chunk)
        if last > 2:
            lax.fori_loop(max(first, 2), last, one, jnp.int32(0))

    def of_mask(mask):
        return (1, 2) if mask == 0 else (2 + (mask - 1) * PARTS, 2 + mask * PARTS)

    class Tail:
        def __init__(self, ref, first, count, index_of, ways, sems):
            self.ref, self.first, self.count, self.index_of = ref, first, count, index_of
            self.ways = ways
            self.send_sem, self.recv_sem, self.turn_send, self.turn_recv = sems

        def source(self, mask):
            return own.at[pl.ds(flipped(group, mask, groups) * channels + self.first, self.count)]

        def at(self, block, time):
            span = pl.ds(pl.multiple_of(time * depth, depth), depth)
            return self.ref.at[self.index_of(block), :, span]

        def turn(self, mask, arriving=False):
            other = flipped(group, mask, groups)
            return pltpu.make_async_remote_copy(
                src_ref=self.source(mask),
                dst_ref=self.at(me, other if arriving else group),
                send_sem=self.turn_send.at[mask],
                recv_sem=self.turn_recv.at[mask],
                device_id={"chan": other},
                device_id_type=MESH,
            )

        def copy(self, block, mask, way, source=None):
            place = self.at(block, flipped(group, mask, groups))
            return pltpu.make_async_remote_copy(
                src_ref=place if source is None else source,
                dst_ref=place,
                send_sem=self.send_sem.at[way[1], self.index_of(block)],
                recv_sem=self.recv_sem.at[self.index_of(block), mask],
                device_id={"inp": way[3]},
                device_id_type=MESH,
            )

        def send(self, block, mask, ways, source=None):
            for way in ways:

                @pl.when(way[2])
                def _(way=way):
                    self.copy(block, mask, way, source).start()

        def pass_on(self, block, mask, exists, ways, origin):
            @pl.when(exists)
            def _():
                self.copy(block, mask, origin).wait_recv()
                self.send(block, mask, ways)

        def drain(self, block, way, cond):
            @pl.when(jnp.logical_and(cond, way[2]))
            def _():
                whole = self.ref.at[self.index_of(block)]
                pltpu.make_async_remote_copy(
                    src_ref=whole,
                    dst_ref=whole,
                    send_sem=self.send_sem.at[way[1], self.index_of(block)],
                    recv_sem=self.recv_sem.at[self.index_of(block), 0],
                    device_id={"inp": way[3]},
                    device_id_type=MESH,
                ).wait_send()

    deferred, line_late, cross_late = [], None, None
    if tails:
        line_late = Tail(line_ref, kept, line_tail, lambda b: b // columns, along_z, tail_sems[:4])
        cross_late = Tail(
            cross_ref, kept + line_tail, cross_tail, lambda b: b, along_x + inner_z, tail_sems[4:]
        )
        deferred = [line_late, cross_late]

    stores = [
        pltpu.make_async_copy(
            own.at[pl.ds(group * channels, kept)],
            all_ref.at[me, :, pl.ds(pl.multiple_of(group * depth, depth), depth)],
            local_sem.at[0],
        )
    ]
    for number, tail in enumerate(deferred):
        stores.append(
            pltpu.make_async_copy(tail.source(0), tail.at(me, group), local_sem.at[1 + number])
        )

    def launch(mask):
        if mask:
            over(*of_mask(mask), lambda c: turn(c).start())
            for tail in deferred:
                tail.turn(mask).start()
        else:
            send(me, 0, along_x + along_z, send_cross, own_part(0))
            send(me, 1, along_z + along_x, send_line, own_part(1))
            for tail in deferred:
                tail.send(me, 0, tail.ways, tail.source(0))
            for store in stores:
                store.start()

    clear = max(0, (frames - TAPS + 1) // PAIR)
    late_halo = jnp.logical_and(group % 2 == 1, has_next)
    ahead = [clear] + [jnp.where(late_halo, clear, 0)] * (groups - 1)

    def loaded(index, carry):
        load(index).wait()
        many = part_rows // strip
        filter_frames(0, clear * PAIR, index * many, (index + 1) * many)
        return carry

    lax.fori_loop(0, LOADS, loaded, jnp.int32(0))
    for mask in range(groups):
        load_rows(mask).wait()
        transform(mask, 0, ahead[mask])

    @pl.when(has_next)
    def _():
        halo.wait_recv()

    filter_frames(clear * PAIR, frames, 0, width // strip)
    for mask in range(groups):
        transform(mask, ahead[mask], frames // PAIR)
        put(mask)
        launch(mask)

    def own_turned(mask):
        def one(chunk):
            turn(chunk, True).wait_recv()
            send(me, chunk, along_z + along_x, send_line)

        over(*of_mask(mask), one)
        for tail in deferred:
            tail.turn(mask, True).wait_recv()
            tail.send(me, mask, tail.ways)

    def late(away, mask):
        if not tails:
            return
        below, above = z >= away, z + away < rows
        line_late.pass_on(me - away * columns, mask, below, (up,), down)
        line_late.pass_on(me + away * columns, mask, above, (down,), up)
        if away == 1:
            cross_late.pass_on(me - 1, mask, x >= 1, inner_z, left)
            cross_late.pass_on(me + 1, mask, x + 1 < columns, inner_z, right)
        below = jnp.logical_and(below, z < rows - 1)
        above = jnp.logical_and(above, z > 0)
        for column in range(columns):
            low = (z - away) * columns + column
            high = (z + away) * columns + column
            cross_late.pass_on(low, mask, below, inner_z[:1], down)
            cross_late.pass_on(high, mask, above, inner_z[1:], up)

    def line(away, first, last):
        below, above = z >= away, z + away < rows

        def one(chunk):
            low, high = along_x + (up,), along_x + (down,)
            if tails and away == 1:
                low, high = cut_x(z == 1) + (up,), cut_x(z == rows - 2) + (down,)
            pass_on(me - away * columns, chunk, below, low, send_line, down)
            pass_on(me + away * columns, chunk, above, high, send_line, up)

        over(first, last, one)

    def cut_x(skip):
        return tuple((n, i, jnp.logical_and(e, jnp.logical_not(skip)), t) for n, i, e, t in along_x)

    def beside(mask):
        if not tails:
            return

        def one(chunk):
            pass_on(me - 1, chunk, jnp.logical_and(at_end, x >= 1), along_z, send_line, left)
            pass_on(
                me + 1, chunk, jnp.logical_and(at_end, x + 1 < columns), along_z, send_line, right
            )

        over(*of_mask(mask), one)

    def crossing(away):
        below, above = z >= away, z + away < rows
        for column in range(columns):
            low = (z - away) * columns + column
            high = (z + away) * columns + column
            pass_on(low, 0, below, (up,), send_cross, down)
            pass_on(high, 0, above, (down,), send_cross, up)

    for away in range(1, columns):
        pass_on(me - away, 0, x >= away, (right,) + along_z, send_cross, left)
        pass_on(me + away, 0, x + away < columns, (left,) + along_z, send_cross, right)
    own_turned(1)
    beside(0)
    crossing(1)
    line(1, *of_mask(0))
    late(1, 0)
    for mask in range(2, groups):
        own_turned(mask)
        beside(mask - 1)
        line(1, *of_mask(mask - 1))
        late(1, mask - 1)
    beside(groups - 1)
    line(1, *of_mask(groups - 1))
    late(1, groups - 1)
    for away in range(2, rows):
        line(away, 1, chunks)
        crossing(away)
        for mask in range(groups):
            late(away, mask)
    for store in stores:
        store.wait()
    outward, sends_out = None, jnp.logical_or(z == 1, z == rows - 2)
    if tails:
        outward = pltpu.make_async_copy(
            cross_ref.at[pl.ds(jnp.where(z == 1, columns, 0), (rows - 1) * columns)],
            outward_ref,
            local_sem.at[3],
        )

        @pl.when(sends_out)
        def _():
            outward.start()

    for away in range(1, columns):
        for row in range(rows):
            before = row * columns + x - away
            after = row * columns + x + away
            due = jnp.logical_not(jnp.logical_and(at_end, z == row)) if tails else True

            def across(chunk):
                pass_on(before, chunk, jnp.logical_and(due, x >= away), (right,), send_line, left)
                pass_on(
                    after, chunk, jnp.logical_and(due, x + away < columns), (left,), send_line, right
                )

            over(1, chunks, across)

    def drain(block, way, cond, to_sems, count):
        @pl.when(jnp.logical_and(cond, way[2]))
        def _():
            whole = all_ref.at[block, pl.ds(0, count)]
            pltpu.make_async_remote_copy(
                src_ref=whole,
                dst_ref=whole,
                send_sem=to_sems.at[way[1], block],
                recv_sem=recv_sem.at[block, 0],
                device_id={"inp": way[3]},
                device_id_type=MESH,
            ).wait_send()

    for row in range(rows):
        for column in range(columns):
            block = row * columns + column
            here, same = x == column, z == row
            carried, over_x = here, True
            if tails:
                carried = jnp.logical_or(here, jnp.logical_and(at_end, same))
                over_x = jnp.logical_and(here, z != {0: 1, rows - 1: rows - 2}.get(row, rows))
            drain(block, up, jnp.logical_and(carried, z >= row), send_line, kept - crossed // groups)
            drain(block, down, jnp.logical_and(carried, z <= row), send_line, kept - crossed // groups)
            across_x = jnp.logical_and(over_x, x >= column)
            drain(block, right, across_x, send_line, kept - crossed // groups)
            across_x = jnp.logical_and(over_x, x <= column)
            drain(block, left, across_x, send_line, kept - crossed // groups)
            drain(block, up, z >= row, send_cross, crossed // groups)
            drain(block, down, z <= row, send_cross, crossed // groups)
            drain(block, right, jnp.logical_and(same, x >= column), send_cross, crossed // groups)
            drain(block, left, jnp.logical_and(same, x <= column), send_cross, crossed // groups)
            if tails:
                if column == 0:
                    own_column = row * columns + x
                    line_late.drain(own_column, up, z >= row)
                    line_late.drain(own_column, down, z <= row)
                cross_late.drain(block, inner_z[0], z >= row)
                cross_late.drain(block, inner_z[1], z <= row)
                cross_late.drain(block, right, jnp.logical_and(same, x >= column))
                cross_late.drain(block, left, jnp.logical_and(same, x <= column))
    over(2, chunks, lambda c: turn(c).wait_send())
    for tail in deferred:
        for mask in range(1, groups):
            tail.turn(mask).wait_send()
    if tails:

        @pl.when(sends_out)
        def _():
            outward.wait()

    @pl.when(has_last)
    def _():
        halo.wait_send()


def grid_of(devices):
    columns = 1 << (int(math.log2(devices)) // 2)
    return devices // columns, columns


def tails_of(devices, channels):
    rows, columns = grid_of(devices)
    if columns != 2 or rows < 4 or channels % 32:
        return 0, 0
    return channels * 3 // 32, channels // 16


def gathered_spectra(voltages):
    width, local_len = voltages.shape
    frames = local_len // L
    devices, groups = lax.axis_size("inp"), lax.axis_size("chan")
    rows, columns = grid_of(devices)
    channels, depth = NCH // groups, 2 * frames
    chunks = 2 + (groups - 1) * PARTS
    line_tail, cross_tail = tails_of(devices, channels)
    kept = channels - line_tail - cross_tail
    share = ((columns - 1) * rows - rows + 1) / (2 * (rows - 1) * (columns - 1))
    crossed = int((0.94 * share - cross_tail / channels) * groups * channels)
    crossed = min(crossed, kept - 16) // 16 * 16
    in_hbm = pl.BlockSpec(memory_space=pl.ANY)

    def blocks(count, some):
        return jax.ShapeDtypeStruct((count, some, groups * depth, width), jnp.bfloat16)

    out_shape, tail_sems = [blocks(devices, kept)], []
    if line_tail:
        out_shape.append(blocks(rows, line_tail))
        out_shape += [blocks(count, cross_tail) for count in (devices, devices - columns)]
        for ways, count in ((2, rows), (4, devices)):
            tail_sems += [
                pltpu.SemaphoreType.DMA((ways, count)),
                pltpu.SemaphoreType.DMA((count, groups)),
                pltpu.SemaphoreType.DMA((groups,)),
                pltpu.SemaphoreType.DMA((groups,)),
            ]
    return pl.pallas_call(
        functools.partial(
            spectra_kernel, (rows, columns, groups, crossed, line_tail, cross_tail)
        ),
        out_shape=out_shape,
        in_specs=[in_hbm, in_hbm, pl.BlockSpec(memory_space=pltpu.VMEM)],
        out_specs=[in_hbm] * len(out_shape),
        scratch_shapes=[
            pltpu.VMEM((width, local_len + (TAPS - 1) * L), jnp.bfloat16),
            pltpu.VMEM((frames * width, L), jnp.bfloat16),
            pltpu.VMEM((2 * NCH, L), jnp.bfloat16),
            pltpu.VMEM((2 * NCH * frames, width), jnp.float32),
            pltpu.VMEM((NCH, depth, width), jnp.bfloat16),
            pltpu.SemaphoreType.DMA((LOADS,)),
            pltpu.SemaphoreType.DMA((groups,)),
            pltpu.SemaphoreType.DMA((2,)),
            pltpu.SemaphoreType.DMA((4,)),
            pltpu.SemaphoreType.DMA((4, devices)),
            pltpu.SemaphoreType.DMA((4, devices)),
            pltpu.SemaphoreType.DMA((devices, chunks)),
            pltpu.SemaphoreType.DMA((chunks,)),
            pltpu.SemaphoreType.DMA((chunks,)),
            *tail_sems,
        ],
        compiler_params=pltpu.CompilerParams(
            collective_id=0, has_side_effects=True, vmem_limit_bytes=52 << 20
        ),
        name="spectra",
    )(voltages, jnp.asarray(transform_rows()), jnp.asarray(filter_window()))


def one_source(place_ref, refs, block, channel):
    return refs[0][block, channel]


def by_column(place_ref, refs, block, channel):
    row, columns = block // place_ref[3], place_ref[3]
    mine = block - row * columns == place_ref[1]
    return jnp.where(mine, refs[0][row, channel], refs[1][row, channel])


def by_row(place_ref, refs, block, channel):
    index = block - place_ref[2]
    away = jnp.logical_and(index >= 0, index < place_ref[4])
    sent = refs[1][jnp.clip(index, 0, refs[1].shape[0] - 1), channel]
    return jnp.where(away, sent, refs[0][block, channel])


def tile_kernel(parts, slots, frames, groups, table_ref, place_ref, *refs):
    if len(parts) == 1:
        fill_tiles(parts[0][0], slots, frames, groups, table_ref, place_ref, refs, refs[-1])
        return
    step = pl.program_id(0)
    for fetch, count, first, last in parts:

        @pl.when(jnp.logical_and(step >= first, step < last))
        def _(fetch=fetch, taken=refs[:count]):
            fill_tiles(fetch, slots, frames, groups, table_ref, place_ref, taken, refs[-1])

        refs = refs[count:]


def fill_tiles(fetch, slots, frames, groups, table_ref, place_ref, taken, out_ref):
    depth = taken[0].shape[2]
    local = depth // (2 * groups)

    def scaled(block, channel):
        rows = fetch(place_ref, taken, block, channel).astype(jnp.float32)
        autopower = jnp.sum(rows * rows, axis=0, keepdims=True) / frames + 1e-06
        return rows * (1.0 / (math.sqrt(frames) * jnp.sqrt(autopower)))

    def one(channel, carry):
        for slot in range(slots):
            first, second = table_ref[slot, 0], table_ref[slot, 1]
            left = scaled(jnp.maximum(first, 0), channel)
            left = jnp.where(first >= 0, left, jnp.zeros_like(left)).astype(jnp.bfloat16)
            right = scaled(jnp.maximum(second, 0), channel).astype(jnp.bfloat16)
            pieces = []
            for start in range(0, depth, 2 * local):
                pieces.append(-right[start + local : start + 2 * local])
                pieces.append(right[start : start + local])
            partner = jnp.concatenate([right, jnp.concatenate(pieces, axis=0)], axis=1)
            out_ref[channel, slot] = lax.dot_general(
                left, partner, (((0,), (0,)), ((), ())), preferred_element_type=jnp.float32
            )
        return carry

    lax.fori_loop(0, out_ref.shape[0], one, jnp.int32(0), unroll=2)


def make_tiles(parts, slot_rows, place, channels, first, tiles=None):
    sources = [source for _, group_sources in parts for source in group_sources]
    counts = [group_sources[0].shape[1] for _, group_sources in parts]
    depth, width = sources[0].shape[2:]
    slots, some = slot_rows.shape[0], sum(counts)
    lanes = max(width, 128)
    held = sum(source.shape[0] for source in sources)
    block_bytes = 2 * held * depth * lanes + 4 * slots * width * max(2 * width, 128)
    group = 16
    while 2 * group * block_bytes > 32 << 20 or any(n % group for n in counts + [first]):
        group -= 1
    offset = first // group
    in_specs, with_steps, start = [], [], 0
    for (fetch, group_sources), count in zip(parts, counts):
        steps = count // group

        def index(c, t, p, start=start, steps=steps):
            return 0, jnp.clip(c - start, 0, steps - 1), 0, 0

        for source in group_sources:
            in_specs.append(pl.BlockSpec((source.shape[0], group, depth, width), index))
        with_steps.append((fetch, len(group_sources), start, start + steps))
        start += steps
    if tiles is not None:
        in_specs.append(pl.BlockSpec(memory_space=pl.ANY))
    return pl.pallas_call(
        functools.partial(
            tile_kernel, with_steps, slots, depth // 2, lax.axis_size("chan")
        ),
        out_shape=jax.ShapeDtypeStruct((channels, slots, width, 2 * width), jnp.float32),
        grid_spec=pltpu.PrefetchScalarGridSpec(
            num_scalar_prefetch=2,
            grid=(some // group,),
            in_specs=in_specs,
            out_specs=pl.BlockSpec(
                (group, slots, width, 2 * width), lambda c, t, p: (offset + c, 0, 0, 0)
            ),
        ),
        input_output_aliases={} if tiles is None else {2 + len(sources): 0},
        compiler_params=pltpu.CompilerParams(vmem_limit_bytes=48 << 20),
        cost_estimate=pl.CostEstimate(
            flops=some * slots * 4 * depth * width * width,
            bytes_accessed=some * (2 * held * depth * width + 8 * slots * width * width),
            transcendentals=0,
        ),
        name="tiles",
    )(slot_rows, place, *sources, *(() if tiles is None else (tiles,)))


def on_device(voltages, tile_table):
    devices, groups = lax.axis_size("inp"), lax.axis_size("chan")
    rows, columns = grid_of(devices)
    channels = NCH // groups
    slot_total = tile_table.shape[0] // devices
    me = lax.axis_index("inp")
    slot_rows = lax.dynamic_slice_in_dim(tile_table, me * slot_total, slot_total, 0)
    z, x = me // columns, me % columns
    at_end = jnp.logical_or(z == 0, z == rows - 1)
    shift = jnp.where(z == 0, columns, 0)
    sent = (rows - 1) * columns
    place = jnp.stack([z, x, shift, jnp.int32(columns), jnp.where(at_end, sent, 0)])
    place = place.astype(jnp.int32)
    main, *late = gathered_spectra(voltages)
    if not late:
        return make_tiles([(one_source, [main])], slot_rows, place, channels, 0)
    by_line, by_cross, outward = late
    over_x = [(i, i // columns * columns + columns - 1 - i % columns) for i in range(devices)]
    to_ends = []
    for column in range(columns):
        to_ends.append((columns + column, column))
        to_ends.append(((rows - 2) * columns + column, (rows - 1) * columns + column))
    line_other = lax.ppermute(by_line, "inp", over_x)
    cross_other = lax.ppermute(outward, "inp", to_ends)
    kept = main.shape[1]
    tiles = make_tiles([(one_source, [main])], slot_rows, place, channels, 0)
    parts = [(by_column, [by_line, line_other]), (by_row, [by_cross, cross_other])]
    return make_tiles(parts, slot_rows, place, channels, kept, tiles)


def solution(mesh):
    placed = (P("inp", "chan"), P())
    return jax.shard_map(
        on_device,
        mesh=mesh,
        in_specs=placed,
        out_specs=P("chan", "inp", None, None),
        check_vma=False,
    )
```
